32 devices in a mesh: box: 4 (over x, core), samp: 8 (over z, y).
Axes of the slice: x: 2, y: 2, z: 4, core: 2. Of those that a mesh axis runs over, the one named last changes fastest.
Arguments:
- child_out: float32 [1024, 2, 18432], P(('box', 'samp')), may hold values from -6 to 6
- child_octant: int32 [128, 8], P(('box', 'samp')), may hold values from 0 to 7, each once within a row
- theta_index: int32 [192, 4], replicated, may hold values from 0 to 95, as said below
- theta_weight: float32 [192, 4], replicated, may hold values from -0.2 to 0.6
- phi_index: int32 [384, 4], replicated, may hold values from 0 to 191, as said below
- phi_weight: float32 [384, 4], replicated, may hold values from -0.2 to 0.6
- shift_angle: float32 [8, 192, 384], replicated, may hold values from -3.140625 to 3.140625
- partner_src: int32 [128, 32], replicated, may hold values from 0 to 127
- partner_disp: int32 [128, 32], replicated, may hold values from 0 to 315
- translation: float32 [316, 2, 192, 384], P(None, None, 'samp'), may hold values from -0.75 to 0.75
Outputs:
- child_in: float32 [1024, 2, 18432], P(('box', 'samp'))
The draws below stay inside these ranges and needn't reach their ends.
Inputs may be any that keep to these rules, and one draw needn't show every extreme that they name: `theta_index`: four stencil indices for each fine theta sample, consecutive coarse samples near it, clipped to the ends so that they may repeat near the poles (repeated weights add). `phi_index`: four consecutive coarse phi samples near each fine phi sample, wrapping around in phi.
All inputs are finite; a program needn't handle non-finite values.
Results may differ from the reference program's by a relative error of at most 0.00007.
Values sent between devices are 32-bit elements; how exact they have to be, the bound alone decides.
A program may use at most 256 MiB of HBM per device.

```python
import jax
import jax.numpy as jnp
from jax import lax

NT1 = 96
NP1 = 192
NT2 = 192
NP2 = 384
NDISP = 316
NPART = 32
NB1 = 1024
NB2 = 128


def draw_theta_index(key, part):
    rows = jnp.arange(NT2, dtype=jnp.int32)
    offset = jax.random.randint(key, (NT2, 1), 0, 3, dtype=jnp.int32)
    start = (rows * NT1 // NT2)[:, None] - 2 + offset
    return jnp.clip(start + jnp.arange(4, dtype=jnp.int32)[None, :], 0, NT1 - 1).astype(jnp.int32)


def draw_phi_index(key, part):
    rows = jnp.arange(NP2, dtype=jnp.int32)
    offset = jax.random.randint(key, (NP2, 1), 0, 3, dtype=jnp.int32)
    start = (rows * NP1 // NP2)[:, None] - 2 + offset
    return jnp.mod(start + jnp.arange(4, dtype=jnp.int32)[None, :], NP1).astype(jnp.int32)


def place_ends(values, own_key, smallest, largest):
    dims = values.shape
    spot = [jax.random.randint(jax.random.fold_in(own_key, axis), (), 0, dims[axis]) for axis in range(len(dims))]
    values = values.at[tuple(spot)].set(smallest)
    longest = dims.index(max(dims))
    spot[longest] = (spot[longest] + 1) % dims[longest]
    return values.at[tuple(spot)].set(largest)


def level_of(key, dims, pieces, low, top_value):
    loudness = 1.0
    for dim, blocks in pieces:
        heights = jax.random.uniform(jax.random.fold_in(jax.random.fold_in(key, 6), dim), (blocks,), jnp.float32, low / len(pieces), top_value / len(pieces))
        loudness = loudness * jnp.repeat(jnp.exp(heights), dims[dim] // blocks).reshape((-1,) + (1,) * (len(dims) - 1 - dim))
    return loudness


def gaussian(key, extent, deviation, reach, pieces=(), kind=jnp.bfloat16):
    level = level_of(key, extent, pieces, -0.22, 0.18) if pieces else 1.0
    entries = jax.random.normal(key, extent, jnp.float32) * deviation * level
    return jnp.minimum(jnp.maximum(entries, -reach), reach).astype(kind)


def setup_inputs(seed: int = 0) -> dict:
    arg_keys = jax.random.split(jax.random.key(seed), 11)
    child_out = gaussian(arg_keys[0], (NB1, 2, NT1 * NP1), 1.0, 6.0, ((0, 32),), jnp.float32)
    child_octant = jax.vmap(lambda own: jax.random.permutation(own, 8))(jax.random.split(arg_keys[1], NB2)).reshape((NB2, 8)).astype(jnp.int32)
    theta_index = draw_theta_index(jax.random.fold_in(arg_keys[10], 71), 0)
    theta_weight = jnp.clip(jax.random.uniform(arg_keys[3], (NT2, 4), jnp.float32, -0.2, 0.6), -0.2, 0.6)
    phi_index = draw_phi_index(jax.random.fold_in(arg_keys[10], 71), 0)
    phi_weight = jnp.clip(jax.random.uniform(arg_keys[5], (NP2, 4), jnp.float32, -0.2, 0.6), -0.2, 0.6)
    shift_angle = jnp.clip(jax.random.uniform(arg_keys[6], (8, NT2, NP2), jnp.float32, -3.140625, 3.140625), -3.140625, 3.140625)
    partner_src = place_ends(jax.random.randint(arg_keys[7], (NB2, NPART), 0, NB2), jax.random.fold_in(arg_keys[7], 1), 0, NB2 - 1).astype(jnp.int32)
    partner_disp = place_ends(jax.random.randint(arg_keys[8], (NB2, NPART), 0, NDISP), jax.random.fold_in(arg_keys[8], 1), 0, NDISP - 1).astype(jnp.int32)
    translation = gaussian(arg_keys[9], (NDISP, 2, NT2, NP2), (1.0 / (2 * NPART) ** 0.5), 0.75, ((2, 8),), jnp.float32)
    return dict(child_out=child_out, child_octant=child_octant, theta_index=theta_index, theta_weight=theta_weight, phi_index=phi_index, phi_weight=phi_weight, shift_angle=shift_angle, partner_src=partner_src, partner_disp=partner_disp, translation=translation)


PRECISE = lax.Precision.HIGHEST


def stencil(index, weight, count):
    hits = (index[:, :, None] == jnp.arange(count, dtype=jnp.int32)[None, None, :]).astype(weight.dtype)
    return jnp.sum(weight[:, :, None] * hits, axis=1)


def spread(field, theta_mat, phi_mat):
    wider = jnp.einsum("czap,qp->czaq", field, phi_mat, precision=PRECISE)
    return jnp.einsum("ta,czaq->cztq", theta_mat, wider, precision=PRECISE)


def contract(field, theta_mat, phi_mat):
    narrow = jnp.einsum("ta,cztq->czaq", theta_mat, field, precision=PRECISE)
    return jnp.einsum("czaq,qp->czap", narrow, phi_mat, precision=PRECISE)


def rotate(field, cosine, sine_part):
    real_part = field[:, 0]
    imag_part = field[:, 1]
    return jnp.stack([real_part * cosine - imag_part * sine_part, real_part * sine_part + imag_part * cosine], axis=1)


def rotate_back(field, cosine, sine_part):
    real_part = field[:, 0]
    imag_part = field[:, 1]
    return jnp.stack([real_part * cosine + imag_part * sine_part, imag_part * cosine - real_part * sine_part], axis=1)


def reference(child_out, child_octant, theta_index, theta_weight, phi_index, phi_weight, shift_angle, partner_src, partner_disp, translation):
    theta_mat = stencil(theta_index, theta_weight, NT1)
    phi_mat = stencil(phi_index, phi_weight, NP1)
    cos_table = jnp.cos(shift_angle)
    sin_table = jnp.sin(shift_angle)
    children = child_out.reshape(NB2, 8, 2, NT1, NP1)

    def aggregate(items):
        kids, octants = items
        cos_sel = jnp.take(cos_table, octants, axis=0)
        sin_sel = jnp.take(sin_table, octants, axis=0)
        fine_child = rotate(spread(kids, theta_mat, phi_mat), cos_sel, sin_sel)
        return jnp.sum(fine_child, axis=0)

    parent_out = lax.map(aggregate, (children, child_octant))

    def translate_one(items):
        sources, displacements = items
        picked = jnp.take(parent_out, sources, axis=0)
        operators = jnp.take(translation, displacements, axis=0)
        real_sum = jnp.sum(operators[:, 0] * picked[:, 0] - operators[:, 1] * picked[:, 1], axis=0)
        imag_sum = jnp.sum(operators[:, 0] * picked[:, 1] + operators[:, 1] * picked[:, 0], axis=0)
        return jnp.stack([real_sum, imag_sum], axis=0)

    parent_in = lax.map(translate_one, (partner_src, partner_disp))

    def disaggregate(items):
        parent, octants = items
        cos_sel = jnp.take(cos_table, octants, axis=0)
        sin_sel = jnp.take(sin_table, octants, axis=0)
        repeated = jnp.broadcast_to(parent[None], (8,) + parent.shape)
        return contract(rotate_back(repeated, cos_sel, sin_sel), theta_mat, phi_mat)

    child_in = lax.map(disaggregate, (parent_in, child_octant))
    return child_in.reshape(NB1, 2, NT1 * NP1)
```

```python
import functools

import jax
import jax.numpy as jnp
from jax import lax
from jax.experimental import pallas as pl
from jax.experimental.pallas import tpu as pltpu
from jax.sharding import PartitionSpec as P

NT1 = 96
NP1 = 192
LANES = 128
MESH = pl.DeviceIdType.MESH
VMEM_LIMIT = 62 * 1024 * 1024


def split(values):
    high = values.astype(jnp.bfloat16)
    low = (values - high.astype(jnp.float32)).astype(jnp.bfloat16)
    return high, low


def dot(left, right):
    return jnp.dot(left, right, preferred_element_type=jnp.float32)


def stencil(wanted, index, weight, axis):
    total = jnp.zeros(wanted.shape, jnp.float32)
    for j in range(index.shape[axis]):
        one = slice(j, j + 1)
        spot = (slice(None), one) if axis == 1 else (one, slice(None))
        total = total + jnp.where(wanted == index[spot], weight[spot], 0.0)
    return total


def iota(shape, axis):
    return lax.broadcasted_iota(jnp.int32, shape, axis)


HALF_PI = (1.5703125, 4.837512969970703e-4, 7.54978995489188e-8)


def cos_sin(angle):
    turns = jnp.floor(angle * 0.6366197723675814 + 0.5)
    rest = ((angle - turns * HALF_PI[0]) - turns * HALF_PI[1]) - turns * HALF_PI[2]
    square = rest * rest
    sine = -1.9515295891e-4 * square + 8.3321608736e-3
    sine = (sine * square - 1.6666654611e-1) * square * rest + rest
    cosine = 2.443315711809948e-5 * square - 1.388731625493765e-3
    cosine = (cosine * square + 4.166664568298827e-2) * square * square - 0.5 * square + 1.0
    half = jnp.floor(turns * 0.5)
    odd = turns - 2.0 * half > 0.5
    flip = half - 2.0 * jnp.floor(half * 0.5) > 0.5
    sin_part = jnp.where(odd, cosine, sine)
    cos_part = jnp.where(odd, -sine, cosine)
    return jnp.where(flip, -cos_part, cos_part), jnp.where(flip, -sin_part, sin_part)


def step_kernel(
    boxes,
    samps,
    partners,
    src_rows,
    disp_rows,
    octant,
    theta_index_t,
    theta_weight_t,
    phi_index_t,
    phi_weight_t,
    child,
    angle,
    table,
    result,
    field,
    wide,
    wide_out,
    grid_sum,
    theta_up,
    theta_down,
    *scratch,
):
    half = NT1 // 2
    width = 2 * NP1
    chunks = angle.shape[2] // LANES
    rows2 = angle.shape[1]
    sources = scratch[:chunks]
    operators = scratch[chunks : 2 * chunks]
    results = scratch[2 * chunks : 3 * chunks]
    outgoing = scratch[3 * chunks : 4 * chunks]
    incoming = scratch[4 * chunks : 5 * chunks]
    cosines = scratch[5 * chunks : 6 * chunks]
    sines = scratch[6 * chunks : 7 * chunks]
    (
        child_sem,
        angle_sem,
        result_sem,
        load_sem,
        own_sem,
        out_send,
        out_recv,
        box_send,
        box_recv,
        back_own,
        back_send,
        back_recv,
    ) = scratch[7 * chunks :]
    per_device, parts = outgoing[0].shape[:2]
    kids = child.shape[0] // per_device
    per_row = width // LANES
    theta_rows = rows2 // samps
    edge = -(-(width // 2) // LANES) * LANES
    gap = edge - width // 2
    group = lax.axis_index("box")
    me = lax.axis_index("samp")
    bits = [1 << i for i in range(boxes.bit_length() - 1)][::-1]

    def mate(bit):
        return group + bit - 2 * bit * lax.rem(lax.div(group, bit), 2)

    barrier = pltpu.get_barrier_semaphore()
    for step in range(1, samps):
        pl.semaphore_signal(barrier, inc=1, device_id=(group, lax.rem(me + step, samps)), device_id_type=MESH)
    for bit in bits:
        pl.semaphore_signal(barrier, inc=1, device_id=(mate(bit), me), device_id_type=MESH)

    def load(chunk):
        return pltpu.make_async_copy(
            table.at[:, :, :, pl.ds(chunk * LANES, LANES)], operators[chunk], load_sem.at[chunk]
        )

    def held_by(box, samp):
        return pl.ds((box * samps + samp) * per_device, per_device)

    def held_in(box):
        return pl.ds(box * samps * per_device, samps * per_device)

    def keep(chunk):
        return pltpu.make_async_copy(
            outgoing[chunk].at[:, :, me], sources[chunk].at[held_by(group, me)], own_sem.at[chunk]
        )

    def out_part(chunk, parent, peer):
        return pltpu.make_async_remote_copy(
            src_ref=outgoing[chunk].at[parent, :, peer],
            dst_ref=sources[chunk].at[(group * samps + me) * per_device + parent],
            send_sem=out_send.at[chunk, peer],
            recv_sem=out_recv.at[chunk, me],
            device_id=(group, peer),
            device_id_type=MESH,
        )

    def out_copy(chunk, peer, owner):
        return pltpu.make_async_remote_copy(
            src_ref=outgoing[chunk].at[:, :, peer],
            dst_ref=sources[chunk].at[held_by(group, owner)],
            send_sem=out_send.at[chunk, peer],
            recv_sem=out_recv.at[chunk, owner],
            device_id=(group, peer),
            device_id_type=MESH,
        )

    def back_slot(chunk, slot):
        return chunk + (slot if chunk == chunks - 1 else 0)

    def back_part(chunk, slot, peer, owner):
        return pltpu.make_async_remote_copy(
            src_ref=results[chunk].at[peer, slot],
            dst_ref=incoming[chunk].at[slot, :, owner],
            send_sem=back_send.at[chunk, peer],
            recv_sem=back_recv.at[back_slot(chunk, slot), owner],
            device_id=(group, peer),
            device_id_type=MESH,
        )

    def back_copy(chunk, peer, owner):
        return pltpu.make_async_remote_copy(
            src_ref=results[chunk].at[peer],
            dst_ref=incoming[chunk].at[:, :, owner],
            send_sem=back_send.at[chunk, peer],
            recv_sem=back_recv.at[chunk, owner],
            device_id=(group, peer),
            device_id_type=MESH,
        )

    def back_keep(chunk):
        return pltpu.make_async_copy(
            results[chunk].at[me], incoming[chunk].at[:, :, me], back_own.at[chunk]
        )

    def box_plan():
        plan = []
        held = [0]
        for bit in bits:
            plan.append((bit, list(held)))
            held = held + [h + bit for h in held]
        return plan

    plan = box_plan()

    def owner_of(mask):
        spot = group
        for bit in bits:
            if mask & bit:
                spot = spot + bit - 2 * bit * lax.rem(lax.div(group, bit), 2)
        return spot

    def hop(chunk, bit, mask):
        return pltpu.make_async_remote_copy(
            src_ref=sources[chunk].at[held_in(owner_of(mask))],
            dst_ref=sources[chunk].at[held_in(owner_of(mask))],
            send_sem=box_send.at[chunk, mask + bit],
            recv_sem=box_recv.at[chunk, mask + bit],
            device_id=(mate(bit), me),
            device_id_type=MESH,
        )

    def hop_arrival(chunk, mask):
        spot = owner_of(mask)
        return pltpu.make_async_remote_copy(
            src_ref=sources[chunk].at[held_in(spot)],
            dst_ref=sources[chunk].at[held_in(spot)],
            send_sem=box_send.at[chunk, mask],
            recv_sem=box_recv.at[chunk, mask],
            device_id=(mate(bits[0]), me),
            device_id_type=MESH,
        )

    def load_angle(chunk):
        return pltpu.make_async_copy(
            angle.at[:, :, pl.ds(chunk * LANES, LANES)], cosines[chunk], angle_sem.at[chunk]
        )

    load_child = pltpu.make_async_copy(child, field, child_sem)

    def tile(parent, part, place):
        return (
            pl.ds(parent * kids, kids),
            pl.ds(place * parts + part, half, stride=per_row * parts),
            slice(None),
        )

    def give(parent):
        rows = pl.ds(parent * kids, kids)
        return pltpu.make_async_copy(field.at[rows], result.at[rows], result_sem.at[parent])

    def build_theta():
        spot = iota((2 * half, rows2), 0)
        sample = jnp.where(spot < half, 2 * spot, 2 * (spot - half) + 1)
        narrow = stencil(sample, theta_index_t, theta_weight_t, 0)
        high, low = split(narrow.T)
        theta_up[:, : 2 * half] = high
        theta_up[:, 2 * half : 4 * half] = high
        theta_up[:, 4 * half :] = low
        high, low = split(narrow)
        theta_down[: 2 * half] = high
        theta_down[2 * half :] = low

    def turn(chunk):
        def one(spot, carry):
            cos_part, sin_part = cos_sin(cosines[chunk][spot])
            cosines[chunk][spot] = cos_part
            sines[chunk][spot] = sin_part
            return carry

        lax.fori_loop(0, cosines[chunk].shape[0], one, 0)

    middle = max(1, samps // 2)
    rim = max(1, samps // 4)
    outer = jnp.logical_or(me < rim, me >= samps - rim)

    def far(peer):
        return lax.div(peer, middle) != lax.div(me, middle)

    def send_out(chunk, parent):
        def one(step, carry):
            peer = lax.rem(me + step, samps)
            if chunk == 0:
                out_part(chunk, parent, peer).start()
            else:

                @pl.when(jnp.logical_not(jnp.logical_and(outer, far(peer))))
                def _():
                    out_part(chunk, parent, peer).start()

            return carry

        lax.fori_loop(1, samps, one, 0)

    def send_far(chunk):
        def one(step, carry):
            peer = lax.rem(me + step, samps)

            @pl.when(jnp.logical_and(outer, far(peer)))
            def _():
                out_copy(chunk, peer, me).start()

            return carry

        lax.fori_loop(1, samps, one, 0)

    def send_last(chunk):
        send_out(chunk, per_device - 1)
        keep(chunk).start()

    def aggregate(chunk):
        lanes = slice(chunk * LANES, (chunk + 1) * LANES)
        sample = iota((edge, LANES), 0)
        mats = []
        for shift in (0, gap):
            high, low = split(stencil(sample - shift, phi_index_t[:, lanes], phi_weight_t[:, lanes], 0))
            mats.append(jnp.concatenate([high, low], axis=1))

        def one_parent(parent, carry):
            block = jnp.concatenate(
                [
                    jnp.concatenate(
                        [field[tile(parent, part, place)].reshape(kids * half, LANES) for place in range(per_row)],
                        axis=1,
                    )
                    for part in range(parts)
                ],
                axis=0,
            )
            pieces = []
            for mat, start in zip(mats, (0, width - edge)):
                high, low = split(block[:, start : start + edge])
                both = dot(high, mat)
                pieces.append(split(both[:, :LANES] + (both[:, LANES:] + dot(low, mat[:, :LANES]))))
            even, odd = pieces
            for slot, piece in enumerate((even[0], odd[0], even[1], odd[1], even[0], odd[0])):
                piece = piece.reshape(parts, kids, half, LANES)
                for part in range(parts):
                    wide[:, slot * half : (slot + 1) * half, part * LANES : (part + 1) * LANES] = piece[part]
            grid_sum[...] = jnp.zeros_like(grid_sum)

            @pl.when(parent > 0)
            def _():
                send_out(chunk, parent - 1)

            def one_child(kid, inner):
                spot = octant[parent, kid]
                fine = dot(theta_up[...], wide[kid])
                real, imag = fine[:, :LANES], fine[:, LANES:]
                cos_part = cosines[chunk][spot]
                sin_part = sines[chunk][spot]
                grid_sum[0] += real * cos_part - imag * sin_part
                grid_sum[1] += real * sin_part + imag * cos_part
                return inner

            lax.fori_loop(0, kids, one_child, 0)
            for part in range(parts):
                for owner in range(samps):
                    outgoing[chunk][parent, part, owner] = grid_sum[
                        part, owner * theta_rows : (owner + 1) * theta_rows
                    ]
            return carry

        lax.fori_loop(0, per_device, one_parent, 0)

    def disaggregate(chunk, first, last):
        rows = slice(chunk * LANES, (chunk + 1) * LANES)
        sample = iota((edge, LANES), 0)
        mats = []
        for shift in (0, gap):
            high, low = split(stencil(sample - shift, phi_index_t[:, rows], phi_weight_t[:, rows], 0).T)
            mats.append((jnp.concatenate([high, high], axis=0), low))

        def one_parent(parent, carry):
            if last:
                returned_part(chunk, parent)
            for part in range(parts):
                for owner in range(samps):
                    grid_sum[part, owner * theta_rows : (owner + 1) * theta_rows] = incoming[chunk][
                        parent, part, owner
                    ]

            def one_child(kid, inner):
                spot = octant[parent, kid]
                real, imag = grid_sum[0], grid_sum[1]
                cos_part = cosines[chunk][spot]
                sin_part = sines[chunk][spot]
                turned = jnp.concatenate(
                    [real * cos_part + imag * sin_part, imag * cos_part - real * sin_part], axis=1
                )
                high, low = split(turned)
                both = dot(theta_down[...], high)
                narrow = both[: 2 * half] + (both[2 * half :] + dot(theta_down[: 2 * half], low))
                for place, piece in enumerate(split(narrow)):
                    for parity in range(2):
                        for part in range(parts):
                            wide_out[
                                parity, kid * parts + part, :, place * LANES : (place + 1) * LANES
                            ] = piece[parity * half : (parity + 1) * half, part * LANES : (part + 1) * LANES]
                return inner

            lax.fori_loop(0, kids, one_child, 0)
            ends = []
            for parity in range(2):
                flat = wide_out[parity].reshape(kids * parts * half, 2 * LANES)
                ends.append(dot(flat, mats[parity][0]) + dot(flat[:, :LANES], mats[parity][1]))
            left, right = ends
            shared = 2 * edge - width
            joined = jnp.concatenate(
                [left[:, : edge - shared], left[:, edge - shared :] + right[:, :shared], right[:, shared:]],
                axis=1,
            ).reshape(kids, parts, half, width)
            for part in range(parts):
                for place in range(per_row):
                    spot = tile(parent, part, place)
                    piece = joined[:, part, :, place * LANES : (place + 1) * LANES]
                    if first:
                        field[spot] = piece
                    else:
                        field[spot] = field[spot] + piece
            if last:

                @pl.when(parent > 0)
                def _():
                    give(parent - 1).start()

            return carry

        lax.fori_loop(0, per_device, one_parent, 0)

    def arrive_and_share(chunk):
        def arrived(step, carry):
            peer = lax.rem(me + samps - step, samps)
            out_copy(chunk, peer, peer).wait_recv()
            return carry

        keep(chunk).wait()
        lax.fori_loop(1, samps, arrived, 0)
        for bit, held in plan:
            hop(chunk, bit, 0).start()

    def pass_on(chunk):
        for position, (bit, held) in enumerate(plan):
            for mask in held:
                if mask == 0:
                    continue
                hop(chunk, bit, mask).start()
            if position + 1 < len(plan):
                for mask in [h + bit for h in held]:
                    hop_arrival(chunk, mask).wait_recv()

    def translate(chunk):
        last_bit, last_held = plan[-1]
        for mask in [h + last_bit for h in last_held]:
            hop_arrival(chunk, mask).wait_recv()
        load(chunk).wait()

        def receivers(slot, carry):
            def one(step, inner):
                peer = lax.rem(me + 1 + step, samps)
                row = (group * samps + peer) * per_device + slot
                real = jnp.zeros(results[chunk].shape[3:], jnp.float32)
                imag = jnp.zeros(results[chunk].shape[3:], jnp.float32)
                for q in range(partners):
                    source = src_rows[q, row]
                    which = disp_rows[q, row]
                    a = sources[chunk][source, 0]
                    b = sources[chunk][source, 1]
                    c = operators[chunk][which, 0]
                    d = operators[chunk][which, 1]
                    real = real + (c * a - d * b)
                    imag = imag + (c * b + d * a)
                results[chunk][peer, slot, 0] = real
                results[chunk][peer, slot, 1] = imag

                @pl.when(step > 0)
                def _():
                    back_part(chunk, slot, lax.rem(me + step, samps), me).start()

                return inner

            lax.fori_loop(0, samps, one, 0)
            return carry

        lax.fori_loop(0, per_device, receivers, 0)

    def returned(chunk):
        def one(step, carry):
            there = lax.rem(me + samps - step, samps)
            back_copy(chunk, there, there).wait_recv()
            return carry

        if chunk < chunks - 1:
            lax.fori_loop(1, samps, one, 0)
        back_keep(chunk).wait()

    def returned_part(chunk, parent):
        def one(step, carry):
            there = lax.rem(me + samps - step, samps)
            back_part(chunk, parent, there, there).wait_recv()
            return carry

        lax.fori_loop(1, samps, one, 0)

    load_angle(0).start()
    load_child.start()
    build_theta()
    load_angle(0).wait()
    turn(0)
    load_child.wait()
    for chunk in range(1, chunks):
        load_angle(chunk).start()
    for chunk in range(chunks):
        load(chunk).start()
    pl.semaphore_wait(barrier, samps - 1 + len(bits))
    aggregate(0)
    for chunk in range(1, chunks):
        load_angle(chunk).wait()
        turn(chunk)
        send_last(chunk - 1)
        if chunk > 1:
            send_far(chunk - 1)
            arrive_and_share(chunk - 2)
        aggregate(chunk)
    send_last(chunks - 1)
    shared = max(0, chunks - 2)
    for chunk in range(chunks):
        early = chunk < shared
        if early:
            pass_on(chunk)
        if chunk == 0 and chunks > 1:
            send_far(chunks - 1)
        if shared < chunks:
            arrive_and_share(shared)
            shared += 1
        if not early:
            pass_on(chunk)
        if chunk:
            back_keep(chunk - 1).start()
        translate(chunk)
    for chunk in range(chunks):
        if chunk == chunks - 1 and chunks == 1:
            back_keep(chunk).start()
        returned(chunk)
        disaggregate(chunk, chunk == 0, chunk == chunks - 1)
        if chunk == 0 and chunks > 1:
            back_keep(chunks - 1).start()
    give(per_device - 1).start()

    for chunk in range(chunks):

        def finish(step, carry, chunk=chunk):
            there = lax.rem(me + step, samps)
            out_copy(chunk, there, there).wait_send()
            back_copy(chunk, there, there).wait_send()
            return carry

        lax.fori_loop(1, samps, finish, 0)
        for bit, held in plan:
            for mask in held:
                hop(chunk, bit, mask).wait_send()
    for parent in range(per_device):
        give(parent).wait()


def local(
    boxes,
    samps,
    child_out,
    child_octant,
    theta_index,
    theta_weight,
    phi_index,
    phi_weight,
    shift_angle,
    partner_src,
    partner_disp,
    translation,
):
    child_count, parts, samples = child_out.shape
    parents, kids = child_octant.shape
    octant_count, rows2, cols2 = shift_angle.shape
    partners = partner_src.shape[1]
    theta_rows = rows2 // samps
    chunks = cols2 // LANES
    tiles = samples // LANES
    child = child_out.reshape(child_count, parts, tiles, LANES).transpose(0, 2, 1, 3)
    child = child.reshape(child_count, tiles * parts, LANES)
    block = (parents, parts, theta_rows, LANES)
    spread = (parents, parts, samps, theta_rows, LANES)
    turns = (octant_count, rows2, LANES)
    anywhere = pl.BlockSpec(memory_space=pl.ANY)
    scalars = pl.BlockSpec(memory_space=pltpu.SMEM)
    vectors = pl.BlockSpec(memory_space=pltpu.VMEM)
    dma = pltpu.SemaphoreType.DMA

    def per_chunk(shape):
        return [pltpu.VMEM(shape, jnp.float32)] * chunks

    child_in = pl.pallas_call(
        functools.partial(step_kernel, boxes, samps, partners),
        out_shape=jax.ShapeDtypeStruct(child.shape, jnp.float32),
        in_specs=[scalars] * 3 + [vectors] * 4 + [anywhere] * 3,
        out_specs=anywhere,
        scratch_shapes=[
            pltpu.VMEM(child.shape, jnp.float32),
            pltpu.VMEM((kids, 3 * NT1, parts * LANES), jnp.bfloat16),
            pltpu.VMEM((2, kids * parts, NT1 // 2, 2 * LANES), jnp.bfloat16),
            pltpu.VMEM((parts, rows2, LANES), jnp.float32),
            pltpu.VMEM((rows2, 3 * NT1), jnp.bfloat16),
            pltpu.VMEM((2 * NT1, rows2), jnp.bfloat16),
        ]
        + per_chunk((boxes * samps * parents,) + block[1:])
        + per_chunk(translation.shape[:3] + (LANES,))
        + per_chunk((samps,) + block)
        + per_chunk(spread)
        + per_chunk(spread)
        + per_chunk(turns)
        + per_chunk(turns)
        + [
            dma(()),
            dma((chunks,)),
            dma((parents,)),
            dma((chunks,)),
            dma((chunks,)),
            dma((chunks, samps)),
            dma((chunks, samps)),
            dma((chunks, boxes)),
            dma((chunks, boxes)),
            dma((chunks,)),
            dma((chunks, samps)),
            dma((chunks - 1 + parents, samps)),
        ],
        compiler_params=pltpu.CompilerParams(
            collective_id=0, has_side_effects=True, vmem_limit_bytes=VMEM_LIMIT
        ),
    )(
        partner_src.T,
        partner_disp.T,
        child_octant,
        theta_index.T,
        theta_weight.T,
        phi_index.T,
        phi_weight.T,
        child,
        shift_angle,
        translation,
    )
    child_in = child_in.reshape(child_count, tiles, parts, LANES).transpose(0, 2, 1, 3)
    return child_in.reshape(child_count, parts, samples)


def solution(mesh):
    in_specs = (
        P(("box", "samp"), None, None),
        P(("box", "samp"), None),
        P(),
        P(),
        P(),
        P(),
        P(),
        P(),
        P(),
        P(None, None, "samp", None),
    )
    out_specs = P(("box", "samp"), None, None)
    body = functools.partial(local, mesh.shape["box"], mesh.shape["samp"])
    return jax.shard_map(body, mesh=mesh, in_specs=in_specs, out_specs=out_specs, check_vma=False)
```

```python
import functools

import jax
import jax.numpy as jnp
from jax import lax
from jax.experimental import pallas as pl
from jax.experimental.pallas import tpu as pltpu
from jax.sharding import PartitionSpec as P

NT1 = 96
NP1 = 192
LANES = 128
MESH = pl.DeviceIdType.MESH
VMEM_LIMIT = 56 * 1024 * 1024


def split(values):
    high = values.astype(jnp.bfloat16)
    low = (values - high.astype(jnp.float32)).astype(jnp.bfloat16)
    return high, low


def dot(left, right):
    return jnp.dot(left, right, preferred_element_type=jnp.float32)


def stencil(wanted, index, weight, axis):
    total = jnp.zeros(wanted.shape, jnp.float32)
    for j in range(index.shape[axis]):
        one = slice(j, j + 1)
        spot = (slice(None), one) if axis == 1 else (one, slice(None))
        total = total + jnp.where(wanted == index[spot], weight[spot], 0.0)
    return total


def iota(shape, axis):
    return lax.broadcasted_iota(jnp.int32, shape, axis)


HALF_PI = (1.5703125, 4.837512969970703e-4, 7.54978995489188e-8)


def cos_sin(angle):
    turns = jnp.floor(angle * 0.6366197723675814 + 0.5)
    rest = ((angle - turns * HALF_PI[0]) - turns * HALF_PI[1]) - turns * HALF_PI[2]
    square = rest * rest
    sine = -1.9515295891e-4 * square + 8.3321608736e-3
    sine = (sine * square - 1.6666654611e-1) * square * rest + rest
    cosine = 2.443315711809948e-5 * square - 1.388731625493765e-3
    cosine = (cosine * square + 4.166664568298827e-2) * square * square - 0.5 * square + 1.0
    half = jnp.floor(turns * 0.5)
    odd = turns - 2.0 * half > 0.5
    flip = half - 2.0 * jnp.floor(half * 0.5) > 0.5
    sin_part = jnp.where(odd, cosine, sine)
    cos_part = jnp.where(odd, -sine, cosine)
    return jnp.where(flip, -cos_part, cos_part), jnp.where(flip, -sin_part, sin_part)


def step_kernel(
    boxes,
    samps,
    partners,
    src_rows,
    disp_rows,
    octant,
    theta_index_t,
    theta_weight_t,
    phi_index_t,
    phi_weight_t,
    child,
    angle,
    table,
    field,
    wide,
    wide_out,
    grid_sum,
    theta_up,
    theta_down,
    *scratch,
):
    half = NT1 // 2
    width = 2 * NP1
    chunks = angle.shape[2] // LANES
    rows2 = angle.shape[1]
    sources = scratch[:chunks]
    operators = scratch[chunks : 2 * chunks]
    results = scratch[2 * chunks : 3 * chunks]
    outgoing = scratch[3 * chunks : 4 * chunks]
    incoming = scratch[4 * chunks : 5 * chunks]
    cosines = scratch[5 * chunks : 6 * chunks]
    sines = scratch[6 * chunks : 7 * chunks]
    (
        child_sem,
        angle_sem,
        load_sem,
        own_sem,
        out_send,
        out_recv,
        box_send,
        box_recv,
        back_own,
        back_send,
        back_recv,
    ) = scratch[7 * chunks :]
    per_device, parts = outgoing[0].shape[:2]
    kids = child.shape[0] // per_device
    per_row = width // LANES
    theta_rows = rows2 // samps
    edge = -(-(width // 2) // LANES) * LANES
    gap = edge - width // 2
    group = lax.axis_index("box")
    me = lax.axis_index("samp")
    bits = [1 << i for i in range(boxes.bit_length() - 1)][::-1]

    def mate(bit):
        return group + bit - 2 * bit * lax.rem(lax.div(group, bit), 2)

    barrier = pltpu.get_barrier_semaphore()
    for step in range(1, samps):
        pl.semaphore_signal(barrier, inc=1, device_id=(group, lax.rem(me + step, samps)), device_id_type=MESH)
    for bit in bits:
        pl.semaphore_signal(barrier, inc=1, device_id=(mate(bit), me), device_id_type=MESH)

    def load(chunk):
        return pltpu.make_async_copy(
            table.at[:, :, :, pl.ds(chunk * LANES, LANES)], operators[chunk], load_sem.at[chunk]
        )

    def held_by(box, samp):
        return pl.ds((box * samps + samp) * per_device, per_device)

    middle = max(1, samps // 2)
    side = lax.div(me, middle)
    rim = max(1, samps // 4)
    outer = jnp.logical_or(me < rim, me >= samps - rim)

    def held_in(box, part):
        start = side if part == 0 else 1 - side
        return pl.ds((box * samps + start * middle) * per_device, middle * per_device)

    def keep(chunk):
        return pltpu.make_async_copy(
            outgoing[chunk].at[:, :, me], sources[chunk].at[held_by(group, me)], own_sem.at[chunk]
        )

    def out_part(chunk, parent, peer):
        return pltpu.make_async_remote_copy(
            src_ref=outgoing[chunk].at[parent, :, peer],
            dst_ref=sources[chunk].at[(group * samps + me) * per_device + parent],
            send_sem=out_send.at[chunk, peer],
            recv_sem=out_recv.at[chunk, me],
            device_id=(group, peer),
            device_id_type=MESH,
        )

    def out_copy(chunk, peer, owner):
        return pltpu.make_async_remote_copy(
            src_ref=outgoing[chunk].at[:, :, peer],
            dst_ref=sources[chunk].at[held_by(group, owner)],
            send_sem=out_send.at[chunk, peer],
            recv_sem=out_recv.at[chunk, owner],
            device_id=(group, peer),
            device_id_type=MESH,
        )

    def back_slot(chunk, slot):
        return chunk * per_device + slot

    def back_part(chunk, slot, peer, owner):
        return pltpu.make_async_remote_copy(
            src_ref=results[chunk].at[peer, slot],
            dst_ref=incoming[chunk].at[slot, :, owner],
            send_sem=back_send.at[chunk, peer],
            recv_sem=back_recv.at[back_slot(chunk, slot), owner],
            device_id=(group, peer),
            device_id_type=MESH,
        )

    def back_copy(chunk, peer, owner):
        return pltpu.make_async_remote_copy(
            src_ref=results[chunk].at[peer],
            dst_ref=incoming[chunk].at[:, :, owner],
            send_sem=back_send.at[chunk, peer],
            recv_sem=back_recv.at[back_slot(chunk, 0), owner],
            device_id=(group, peer),
            device_id_type=MESH,
        )

    def back_keep(chunk):
        return pltpu.make_async_copy(
            results[chunk].at[me], incoming[chunk].at[:, :, me], back_own.at[chunk]
        )

    def box_plan():
        plan = []
        held = [0]
        for bit in bits:
            plan.append((bit, list(held)))
            held = held + [h + bit for h in held]
        return plan

    plan = box_plan()

    def owner_of(mask):
        spot = group
        for bit in bits:
            if mask & bit:
                spot = spot + bit - 2 * bit * lax.rem(lax.div(group, bit), 2)
        return spot

    def hop(chunk, bit, mask, part):
        spot = held_in(owner_of(mask), part)
        return pltpu.make_async_remote_copy(
            src_ref=sources[chunk].at[spot],
            dst_ref=sources[chunk].at[spot],
            send_sem=box_send.at[chunk, mask + bit, part],
            recv_sem=box_recv.at[chunk, mask + bit, part],
            device_id=(mate(bit), me),
            device_id_type=MESH,
        )

    def hop_arrival(chunk, mask, part):
        spot = held_in(owner_of(mask), part)
        return pltpu.make_async_remote_copy(
            src_ref=sources[chunk].at[spot],
            dst_ref=sources[chunk].at[spot],
            send_sem=box_send.at[chunk, mask, part],
            recv_sem=box_recv.at[chunk, mask, part],
            device_id=(mate(bits[0]), me),
            device_id_type=MESH,
        )

    def load_angle(chunk):
        return pltpu.make_async_copy(
            angle.at[:, :, pl.ds(chunk * LANES, LANES)], cosines[chunk], angle_sem.at[chunk]
        )

    load_child = pltpu.make_async_copy(child, field, child_sem)

    def tile(parent, part, place):
        return (
            pl.ds(parent * kids, kids),
            pl.ds(place * parts + part, half, stride=per_row * parts),
            slice(None),
        )

    def build_theta():
        spot = iota((2 * half, rows2), 0)
        sample = jnp.where(spot < half, 2 * spot, 2 * (spot - half) + 1)
        narrow = stencil(sample, theta_index_t, theta_weight_t, 0)
        high, low = split(narrow.T)
        theta_up[:, : 2 * half] = high
        theta_up[:, 2 * half : 4 * half] = high
        theta_up[:, 4 * half :] = low
        high, low = split(narrow)
        theta_down[: 2 * half] = high
        theta_down[2 * half :] = low

    def turn(chunk):
        def one(spot, carry):
            cos_part, sin_part = cos_sin(cosines[chunk][spot])
            cosines[chunk][spot] = cos_part
            sines[chunk][spot] = sin_part
            return carry

        lax.fori_loop(0, cosines[chunk].shape[0], one, 0)

    def far(peer):
        return lax.div(peer, middle) != side

    def send_out(chunk, parent):
        def one(step, carry):
            peer = lax.rem(me + step, samps)
            if chunk == 0:
                out_part(chunk, parent, peer).start()
            else:

                @pl.when(jnp.logical_not(jnp.logical_and(outer, far(peer))))
                def _():
                    out_part(chunk, parent, peer).start()

            return carry

        lax.fori_loop(1, samps, one, 0)

    def send_far(chunk):
        def one(step, carry):
            peer = lax.rem(me + step, samps)

            @pl.when(jnp.logical_and(outer, far(peer)))
            def _():
                out_copy(chunk, peer, me).start()

            return carry

        lax.fori_loop(1, samps, one, 0)

    def send_last(chunk):
        send_out(chunk, per_device - 1)
        keep(chunk).start()

    def aggregate(chunk, between):
        lanes = slice(chunk * LANES, (chunk + 1) * LANES)
        sample = iota((edge, LANES), 0)
        mats = []
        for shift in (0, gap):
            high, low = split(stencil(sample - shift, phi_index_t[:, lanes], phi_weight_t[:, lanes], 0))
            mats.append(jnp.concatenate([high, low], axis=1))

        def one_parent(parent, carry):
            block = jnp.concatenate(
                [
                    jnp.concatenate(
                        [field[tile(parent, part, place)].reshape(kids * half, LANES) for place in range(per_row)],
                        axis=1,
                    )
                    for part in range(parts)
                ],
                axis=0,
            )
            pieces = []
            for mat, start in zip(mats, (0, width - edge)):
                high, low = split(block[:, start : start + edge])
                both = dot(high, mat)
                pieces.append(split(both[:, :LANES] + (both[:, LANES:] + dot(low, mat[:, :LANES]))))
            even, odd = pieces
            for slot, piece in enumerate((even[0], odd[0], even[1], odd[1], even[0], odd[0])):
                piece = piece.reshape(parts, kids, half, LANES)
                for part in range(parts):
                    wide[:, slot * half : (slot + 1) * half, part * LANES : (part + 1) * LANES] = piece[part]
            grid_sum[...] = jnp.zeros_like(grid_sum)

            if chunk == 0:

                @pl.when(parent == min(1, per_device - 1))
                def _():
                    pl.semaphore_wait(barrier, samps - 1 + len(bits))

            @pl.when(parent > 0)
            def _():
                send_out(chunk, parent - 1)

            if between:

                @pl.when(parent == per_device // 2)
                def _():
                    run(between)

            def one_child(kid, inner):
                spot = octant[parent, kid]
                fine = dot(theta_up[...], wide[kid])
                real, imag = fine[:, :LANES], fine[:, LANES:]
                cos_part = cosines[chunk][spot]
                sin_part = sines[chunk][spot]
                grid_sum[0] += real * cos_part - imag * sin_part
                grid_sum[1] += real * sin_part + imag * cos_part
                return inner

            lax.fori_loop(0, kids, one_child, 0)
            for part in range(parts):
                for owner in range(samps):
                    outgoing[chunk][parent, part, owner] = grid_sum[
                        part, owner * theta_rows : (owner + 1) * theta_rows
                    ]
            return carry

        lax.fori_loop(0, per_device, one_parent, 0)

    def disaggregate(chunk, first):
        rows = slice(chunk * LANES, (chunk + 1) * LANES)
        sample = iota((edge, LANES), 0)
        mats = []
        for shift in (0, gap):
            high, low = split(stencil(sample - shift, phi_index_t[:, rows], phi_weight_t[:, rows], 0).T)
            mats.append((jnp.concatenate([high, high], axis=0), low))

        def one_parent(parent, carry):
            returned_part(chunk, parent)
            for part in range(parts):
                for owner in range(samps):
                    grid_sum[part, owner * theta_rows : (owner + 1) * theta_rows] = incoming[chunk][
                        parent, part, owner
                    ]

            def one_child(kid, inner):
                spot = octant[parent, kid]
                real, imag = grid_sum[0], grid_sum[1]
                cos_part = cosines[chunk][spot]
                sin_part = sines[chunk][spot]
                turned = jnp.concatenate(
                    [real * cos_part + imag * sin_part, imag * cos_part - real * sin_part], axis=1
                )
                high, low = split(turned)
                both = dot(theta_down[...], high)
                narrow = both[: 2 * half] + (both[2 * half :] + dot(theta_down[: 2 * half], low))
                for place, piece in enumerate(split(narrow)):
                    for parity in range(2):
                        for part in range(parts):
                            wide_out[
                                parity, kid * parts + part, :, place * LANES : (place + 1) * LANES
                            ] = piece[parity * half : (parity + 1) * half, part * LANES : (part + 1) * LANES]
                return inner

            lax.fori_loop(0, kids, one_child, 0)
            ends = []
            for parity in range(2):
                flat = wide_out[parity].reshape(kids * parts * half, 2 * LANES)
                ends.append(dot(flat, mats[parity][0]) + dot(flat[:, :LANES], mats[parity][1]))
            left, right = ends
            shared = 2 * edge - width
            joined = jnp.concatenate(
                [left[:, : edge - shared], left[:, edge - shared :] + right[:, :shared], right[:, shared:]],
                axis=1,
            ).reshape(kids, parts, half, width)
            for part in range(parts):
                for place in range(per_row):
                    spot = tile(parent, part, place)
                    piece = joined[:, part, :, place * LANES : (place + 1) * LANES]
                    if first:
                        field[spot] = piece
                    else:
                        field[spot] = field[spot] + piece
            return carry

        lax.fori_loop(0, per_device, one_parent, 0)

    def share(chunk, part):
        def near_one(step, carry):
            peer = side * middle + lax.rem(me - side * middle + step, middle)
            out_copy(chunk, peer, peer).wait_recv()
            return carry

        def far_one(step, carry):
            peer = (1 - side) * middle + step
            out_copy(chunk, peer, peer).wait_recv()
            return carry

        if part == 0:
            keep(chunk).wait()
            lax.fori_loop(1, middle, near_one, 0)
        else:
            lax.fori_loop(0, middle, far_one, 0)
        for bit, held in plan:
            hop(chunk, bit, 0, part).start()

    def pass_on(chunk, part):
        for position, (bit, held) in enumerate(plan):
            for mask in held:
                if mask == 0:
                    continue
                hop(chunk, bit, mask, part).start()
            if position + 1 < len(plan):
                for mask in [h + bit for h in held]:
                    hop_arrival(chunk, mask, part).wait_recv()

    def back_far(chunk):
        def one(spot, carry):
            slot = lax.div(spot, middle)
            peer = (1 - side) * middle + lax.rem(spot, middle)
            back_part(chunk, slot, peer, me).start()
            return carry

        @pl.when(outer)
        def _():
            lax.fori_loop(0, per_device * middle, one, 0)

    def translate(chunk, between):
        last_bit, last_held = plan[-1]
        for mask in [h + last_bit for h in last_held]:
            for part in range(2):
                hop_arrival(chunk, mask, part).wait_recv()
        load(chunk).wait()

        def receivers(slot, carry):
            if between:

                @pl.when(slot == per_device // 2)
                def _():
                    run(between)

            def one(step, inner):
                peer = lax.rem(me + 1 + step, samps)
                row = (group * samps + peer) * per_device + slot
                real = jnp.zeros(results[chunk].shape[3:], jnp.float32)
                imag = jnp.zeros(results[chunk].shape[3:], jnp.float32)
                for q in range(partners):
                    source = src_rows[q, row]
                    which = disp_rows[q, row]
                    a = sources[chunk][source, 0]
                    b = sources[chunk][source, 1]
                    c = operators[chunk][which, 0]
                    d = operators[chunk][which, 1]
                    real = real + (c * a - d * b)
                    imag = imag + (c * b + d * a)
                results[chunk][peer, slot, 0] = real
                results[chunk][peer, slot, 1] = imag

                there = lax.rem(me + step, samps)

                @pl.when(jnp.logical_and(step > 0, jnp.logical_not(jnp.logical_and(outer, far(there)))))
                def _():
                    back_part(chunk, slot, there, me).start()

                return inner

            lax.fori_loop(0, samps, one, 0)
            return carry

        lax.fori_loop(0, per_device, receivers, 0)

    def returned_part(chunk, parent):
        def one(step, carry):
            there = lax.rem(me + samps - step, samps)
            back_part(chunk, parent, there, there).wait_recv()
            return carry

        lax.fori_loop(1, samps, one, 0)

    load_angle(0).start()
    load_child.start()
    build_theta()
    load_angle(0).wait()
    turn(0)
    load_child.wait()
    for chunk in range(1, chunks):
        load_angle(chunk).start()
    for chunk in range(chunks):
        load(chunk).start()
    called = set()

    def fresh(*calls):
        left = [call for call in calls if 0 <= call[1] < chunks and call not in called]
        called.update(left)
        return left

    def run(calls):
        for function, *rest in calls:
            function(*rest)

    aggregate(0, [])
    for chunk in range(1, chunks):
        load_angle(chunk).wait()
        turn(chunk)
        send_last(chunk - 1)
        if chunk > 1:
            run(fresh((send_far, chunk - 1)))
        run(fresh((share, chunk - 2, 1)))
        aggregate(chunk, fresh((share, chunk - 1, 0), (pass_on, chunk - 2, 0)))
    last = chunks - 1
    send_last(last)
    for chunk in range(chunks):
        if chunk == last:
            run(fresh((pass_on, last, 0), (share, last, 1), (back_far, last - 2)))
        run(fresh((share, chunk, 0), (pass_on, chunk, 0)))
        if chunk == 0 and chunks > 1:
            run(fresh((pass_on, 0, 1)) if chunks > 2 else [])
            run(fresh((send_far, last)))
        run(fresh((share, chunk, 1), (pass_on, chunk, 1)))
        if chunk:
            back_keep(chunk - 1).start()
        translate(chunk, fresh((share, chunk + 1, 1), (share, last, 0)) if chunk + 1 < last else [])
    for chunk in range(last):
        run(fresh((back_far, chunk)))
        if chunk + 1 < last:
            run(fresh((back_far, chunk + 1)))
        back_keep(chunk).wait()
        if chunk + 1 == last:
            run(fresh((back_far, last)))
        if chunk == 0:
            back_keep(last).start()
        disaggregate(chunk, chunk == 0)
    if last == 0:
        run(fresh((back_far, last)))
        back_keep(last).start()
    back_keep(last).wait()

    for chunk in range(chunks):

        def finish(step, carry, chunk=chunk):
            there = lax.rem(me + step, samps)
            out_copy(chunk, there, there).wait_send()
            if chunk < last:
                back_copy(chunk, there, there).wait_send()
            return carry

        lax.fori_loop(1, samps, finish, 0)
        for bit, held in plan:
            for mask in held:
                for part in range(2):
                    hop(chunk, bit, mask, part).wait_send()
    disaggregate(last, last == 0)

    def finish_last(step, carry):
        there = lax.rem(me + step, samps)
        back_copy(last, there, there).wait_send()
        return carry

    lax.fori_loop(1, samps, finish_last, 0)


def local(
    boxes,
    samps,
    child_out,
    child_octant,
    theta_index,
    theta_weight,
    phi_index,
    phi_weight,
    shift_angle,
    partner_src,
    partner_disp,
    translation,
):
    child_count, parts, samples = child_out.shape
    parents, kids = child_octant.shape
    octant_count, rows2, cols2 = shift_angle.shape
    partners = partner_src.shape[1]
    theta_rows = rows2 // samps
    chunks = cols2 // LANES
    tiles = samples // LANES
    child = child_out.reshape(child_count, parts, tiles, LANES).transpose(0, 2, 1, 3)
    child = child.reshape(child_count, tiles * parts, LANES)
    block = (parents, parts, theta_rows, LANES)
    spread = (parents, parts, samps, theta_rows, LANES)
    turns = (octant_count, rows2, LANES)
    anywhere = pl.BlockSpec(memory_space=pl.ANY)
    scalars = pl.BlockSpec(memory_space=pltpu.SMEM)
    vectors = pl.BlockSpec(memory_space=pltpu.VMEM)
    dma = pltpu.SemaphoreType.DMA

    def per_chunk(shape):
        return [pltpu.VMEM(shape, jnp.float32)] * chunks

    child_in = pl.pallas_call(
        functools.partial(step_kernel, boxes, samps, partners),
        out_shape=pltpu.VMEM(child.shape, jnp.float32),
        in_specs=[scalars] * 3 + [vectors] * 4 + [anywhere] * 3,
        out_specs=vectors,
        scratch_shapes=[
            pltpu.VMEM((kids, 3 * NT1, parts * LANES), jnp.bfloat16),
            pltpu.VMEM((2, kids * parts, NT1 // 2, 2 * LANES), jnp.bfloat16),
            pltpu.VMEM((parts, rows2, LANES), jnp.float32),
            pltpu.VMEM((rows2, 3 * NT1), jnp.bfloat16),
            pltpu.VMEM((2 * NT1, rows2), jnp.bfloat16),
        ]
        + per_chunk((boxes * samps * parents,) + block[1:])
        + per_chunk(translation.shape[:3] + (LANES,))
        + per_chunk((samps,) + block)
        + per_chunk(spread)
        + per_chunk(spread)
        + per_chunk(turns)
        + per_chunk(turns)
        + [
            dma(()),
            dma((chunks,)),
            dma((chunks,)),
            dma((chunks,)),
            dma((chunks, samps)),
            dma((chunks, samps)),
            dma((chunks, boxes, 2)),
            dma((chunks, boxes, 2)),
            dma((chunks,)),
            dma((chunks, samps)),
            dma((chunks * parents, samps)),
        ],
        compiler_params=pltpu.CompilerParams(
            collective_id=0, has_side_effects=True, vmem_limit_bytes=VMEM_LIMIT
        ),
    )(
        partner_src.T,
        partner_disp.T,
        child_octant,
        theta_index.T,
        theta_weight.T,
        phi_index.T,
        phi_weight.T,
        child,
        shift_angle,
        translation,
    )
    child_in = child_in.reshape(child_count, tiles, parts, LANES).transpose(0, 2, 1, 3)
    return child_in.reshape(child_count, parts, samples)


def solution(mesh):
    in_specs = (
        P(("box", "samp"), None, None),
        P(("box", "samp"), None),
        P(),
        P(),
        P(),
        P(),
        P(),
        P(),
        P(),
        P(None, None, "samp", None),
    )
    out_specs = P(("box", "samp"), None, None)
    body = functools.partial(local, mesh.shape["box"], mesh.shape["samp"])
    return jax.shard_map(body, mesh=mesh, in_specs=in_specs, out_specs=out_specs, check_vma=False)
```

```python
import functools

import jax
import jax.numpy as jnp
from jax import lax
from jax.experimental import pallas as pl
from jax.experimental.pallas import tpu as pltpu
from jax.sharding import PartitionSpec as P

NT1 = 96
NP1 = 192
LANES = 128
MESH = pl.DeviceIdType.MESH
VMEM_LIMIT = 56 * 1024 * 1024


def split(values):
    high = values.astype(jnp.bfloat16)
    low = (values - high.astype(jnp.float32)).astype(jnp.bfloat16)
    return high, low


def dot(left, right):
    return jnp.dot(left, right, preferred_element_type=jnp.float32)


def stencil(wanted, index, weight, axis):
    total = jnp.zeros(wanted.shape, jnp.float32)
    for j in range(index.shape[axis]):
        one = slice(j, j + 1)
        spot = (slice(None), one) if axis == 1 else (one, slice(None))
        total = total + jnp.where(wanted == index[spot], weight[spot], 0.0)
    return total


def iota(shape, axis):
    return lax.broadcasted_iota(jnp.int32, shape, axis)


HALF_PI = (1.5703125, 4.837512969970703e-4, 7.54978995489188e-8)


def cos_sin(angle):
    turns = jnp.floor(angle * 0.6366197723675814 + 0.5)
    rest = ((angle - turns * HALF_PI[0]) - turns * HALF_PI[1]) - turns * HALF_PI[2]
    square = rest * rest
    sine = -1.9515295891e-4 * square + 8.3321608736e-3
    sine = (sine * square - 1.6666654611e-1) * square * rest + rest
    cosine = 2.443315711809948e-5 * square - 1.388731625493765e-3
    cosine = (cosine * square + 4.166664568298827e-2) * square * square - 0.5 * square + 1.0
    half = jnp.floor(turns * 0.5)
    odd = turns - 2.0 * half > 0.5
    flip = half - 2.0 * jnp.floor(half * 0.5) > 0.5
    sin_part = jnp.where(odd, cosine, sine)
    cos_part = jnp.where(odd, -sine, cosine)
    return jnp.where(flip, -cos_part, cos_part), jnp.where(flip, -sin_part, sin_part)


def step_kernel(
    boxes,
    samps,
    partners,
    src_in,
    disp_in,
    octant_in,
    theta_index_in,
    theta_weight_in,
    phi_index_in,
    phi_weight_in,
    child,
    angle,
    table,
    field,
    wide,
    wide_out,
    grid_sum,
    theta_up,
    theta_down,
    src_rows,
    disp_rows,
    octant,
    theta_index_t,
    theta_weight_t,
    phi_index_t,
    phi_weight_t,
    *scratch,
):
    half = NT1 // 2
    width = 2 * NP1
    chunks = angle.shape[2] // LANES
    rows2 = angle.shape[1]
    sources = scratch[:chunks]
    operators = scratch[chunks : 2 * chunks]
    results = scratch[2 * chunks : 3 * chunks]
    outgoing = scratch[3 * chunks : 4 * chunks]
    incoming = scratch[4 * chunks : 5 * chunks]
    cosines = scratch[5 * chunks : 6 * chunks]
    sines = scratch[6 * chunks : 7 * chunks]
    (
        child_sem,
        angle_sem,
        load_sem,
        out_send,
        out_recv,
        box_send,
        box_recv,
        back_own,
        back_send,
        back_recv,
        small_sem,
    ) = scratch[7 * chunks :]
    per_device, parts = outgoing[0].shape[:2]
    kids = child.shape[0] // per_device
    per_row = width // LANES
    theta_rows = rows2 // samps
    edge = -(-(width // 2) // LANES) * LANES
    gap = edge - width // 2
    group = lax.axis_index("box")
    me = lax.axis_index("samp")
    bits = [1 << i for i in range(boxes.bit_length() - 1)][::-1]

    def mate(bit):
        return group + bit - 2 * bit * lax.rem(lax.div(group, bit), 2)

    barrier = pltpu.get_barrier_semaphore()
    for step in range(1, samps):
        pl.semaphore_signal(barrier, inc=1, device_id=(group, lax.rem(me + step, samps)), device_id_type=MESH)
    for bit in bits:
        pl.semaphore_signal(barrier, inc=1, device_id=(mate(bit), me), device_id_type=MESH)

    def load(chunk):
        return pltpu.make_async_copy(
            table.at[:, :, :, pl.ds(chunk * LANES, LANES)], operators[chunk], load_sem.at[chunk]
        )

    def held_by(box, samp):
        return pl.ds((box * samps + samp) * per_device, per_device)

    middle = max(1, samps // 2)
    side = lax.div(me, middle)
    rim = max(1, samps // 4)
    outer = jnp.logical_or(me < rim, me >= samps - rim)

    def apart(peer):
        return lax.rem(lax.div(peer, middle) + side, 2)

    def held_in(box, part):
        start = side if part == 0 else 1 - side
        return pl.ds((box * samps + start * middle) * per_device, middle * per_device)

    def keep(chunk):
        return pltpu.make_async_copy(
            outgoing[chunk].at[:, :, me], sources[chunk].at[held_by(group, me)], out_recv.at[chunk, 0]
        )

    def out_part(chunk, parent, peer):
        return pltpu.make_async_remote_copy(
            src_ref=outgoing[chunk].at[parent, :, peer],
            dst_ref=sources[chunk].at[(group * samps + me) * per_device + parent],
            send_sem=out_send.at[chunk],
            recv_sem=out_recv.at[chunk, apart(peer)],
            device_id=(group, peer),
            device_id_type=MESH,
        )

    def out_copy(chunk, peer):
        return pltpu.make_async_remote_copy(
            src_ref=outgoing[chunk].at[:, :, peer],
            dst_ref=sources[chunk].at[held_by(group, me)],
            send_sem=out_send.at[chunk],
            recv_sem=out_recv.at[chunk, apart(peer)],
            device_id=(group, peer),
            device_id_type=MESH,
        )

    def back_part(chunk, slot, peer):
        return pltpu.make_async_remote_copy(
            src_ref=results[chunk].at[peer, slot],
            dst_ref=incoming[chunk].at[slot, :, me],
            send_sem=back_send.at[chunk],
            recv_sem=back_recv.at[chunk * per_device + slot],
            device_id=(group, peer),
            device_id_type=MESH,
        )

    def await_bytes(ref, sem):
        pltpu.make_async_copy(ref, ref, sem).wait()

    def back_keep(chunk):
        return pltpu.make_async_copy(
            results[chunk].at[me], incoming[chunk].at[:, :, me], back_own.at[chunk]
        )

    def box_plan():
        plan = []
        held = [0]
        for bit in bits:
            plan.append((bit, list(held)))
            held = held + [h + bit for h in held]
        return plan

    plan = box_plan()

    def owner_of(mask):
        spot = group
        for bit in bits:
            if mask & bit:
                spot = spot + bit - 2 * bit * lax.rem(lax.div(group, bit), 2)
        return spot

    def hop_slot(mask, part):
        return 0 if mask % 2 else mask - 1 + part

    def hop(chunk, bit, mask, part):
        spot = held_in(owner_of(mask), part)
        return pltpu.make_async_remote_copy(
            src_ref=sources[chunk].at[spot],
            dst_ref=sources[chunk].at[spot],
            send_sem=box_send.at[chunk],
            recv_sem=box_recv.at[chunk, hop_slot(mask + bit, part)],
            device_id=(mate(bit), me),
            device_id_type=MESH,
        )

    def load_angle(chunk):
        return pltpu.make_async_copy(
            angle.at[:, :, pl.ds(chunk * LANES, LANES)], cosines[chunk], angle_sem.at[chunk]
        )

    small = [
        pltpu.make_async_copy(source, place, small_sem.at[spot])
        for spot, (source, place) in enumerate(
            (
                (octant_in, octant),
                (theta_index_in, theta_index_t),
                (theta_weight_in, theta_weight_t),
                (phi_index_in, phi_index_t),
                (phi_weight_in, phi_weight_t),
                (src_in, src_rows),
                (disp_in, disp_rows),
            )
        )
    ]
    def load_child(parent):
        rows = pl.ds(parent * kids, kids)
        return pltpu.make_async_copy(child.at[rows], field.at[rows], child_sem.at[parent])

    def tile(parent, part, place):
        return (
            pl.ds(parent * kids, kids),
            pl.ds(place * parts + part, half, stride=per_row * parts),
            slice(None),
        )

    def build_theta():
        spot = iota((2 * half, rows2), 0)
        sample = jnp.where(spot < half, 2 * spot, 2 * (spot - half) + 1)
        narrow = stencil(sample, theta_index_t, theta_weight_t, 0)
        high, low = split(narrow.T)
        theta_up[:, : 2 * half] = high
        theta_up[:, 2 * half : 4 * half] = high
        theta_up[:, 4 * half :] = low
        high, low = split(narrow)
        theta_down[: 2 * half] = high
        theta_down[2 * half :] = low

    def turn(chunk):
        def one(spot, carry):
            cos_part, sin_part = cos_sin(cosines[chunk][spot])
            cosines[chunk][spot] = cos_part
            sines[chunk][spot] = sin_part
            return carry

        lax.fori_loop(0, cosines[chunk].shape[0], one, 0)

    def far(peer):
        return lax.div(peer, middle) != side

    def send_out(chunk, parent):
        def one(step, carry):
            peer = lax.rem(me + step, samps)
            if chunk == 0:
                out_part(chunk, parent, peer).start()
            else:

                @pl.when(jnp.logical_not(jnp.logical_and(outer, far(peer))))
                def _():
                    out_part(chunk, parent, peer).start()

            return carry

        lax.fori_loop(1, samps, one, 0)

    def send_far(chunk):
        def one(step, carry):
            peer = lax.rem(me + step, samps)

            @pl.when(jnp.logical_and(outer, far(peer)))
            def _():
                out_copy(chunk, peer).start()

            return carry

        lax.fori_loop(1, samps, one, 0)

    def send_last(chunk):
        if chunk > 0:
            send_out(chunk, per_device - 1)
        keep(chunk).start()

    def aggregate(chunk, between):
        lanes = slice(chunk * LANES, (chunk + 1) * LANES)
        sample = iota((edge, LANES), 0)
        mats = []
        for shift in (0, gap):
            high, low = split(stencil(sample - shift, phi_index_t[:, lanes], phi_weight_t[:, lanes], 0))
            mats.append(jnp.concatenate([high, low], axis=1))

        def one_parent(parent, carry):
            block = jnp.concatenate(
                [
                    jnp.concatenate(
                        [field[tile(parent, part, place)].reshape(kids * half, LANES) for place in range(per_row)],
                        axis=1,
                    )
                    for part in range(parts)
                ],
                axis=0,
            )
            pieces = []
            for mat, start in zip(mats, (0, width - edge)):
                high, low = split(block[:, start : start + edge])
                both = dot(high, mat)
                pieces.append(split(both[:, :LANES] + (both[:, LANES:] + dot(low, mat[:, :LANES]))))
            even, odd = pieces
            for slot, piece in enumerate((even[0], odd[0], even[1], odd[1], even[0], odd[0])):
                piece = piece.reshape(parts, kids, half, LANES)
                for part in range(parts):
                    wide[:, slot * half : (slot + 1) * half, part * LANES : (part + 1) * LANES] = piece[part]
            grid_sum[...] = jnp.zeros_like(grid_sum)

            if chunk > 0:

                @pl.when(parent > 0)
                def _():
                    send_out(chunk, parent - 1)

            if between:

                @pl.when(parent == per_device // 2)
                def _():
                    run(between)

            def one_child(kid, inner):
                spot = octant[parent, kid]
                fine = dot(theta_up[...], wide[kid])
                real, imag = fine[:, :LANES], fine[:, LANES:]
                cos_part = cosines[chunk][spot]
                sin_part = sines[chunk][spot]
                grid_sum[0] += real * cos_part - imag * sin_part
                grid_sum[1] += real * sin_part + imag * cos_part
                return inner

            lax.fori_loop(0, kids, one_child, 0)
            for part in range(parts):
                for owner in range(samps):
                    outgoing[chunk][parent, part, owner] = grid_sum[
                        part, owner * theta_rows : (owner + 1) * theta_rows
                    ]
            if chunk == 0:

                @pl.when(parent == 0)
                def _():
                    pl.semaphore_wait(barrier, samps - 1 + len(bits))

                send_out(chunk, parent)
            return carry

        lax.fori_loop(0, per_device, one_parent, 0)

    def disaggregate(chunk, first, between):
        rows = slice(chunk * LANES, (chunk + 1) * LANES)
        sample = iota((edge, LANES), 0)
        mats = []
        for shift in (0, gap):
            high, low = split(stencil(sample - shift, phi_index_t[:, rows], phi_weight_t[:, rows], 0).T)
            mats.append((jnp.concatenate([high, high], axis=0), low))

        def one_parent(parent, carry):
            returned_part(chunk, parent)
            for function, *rest in between:
                function(*rest, parent)
            for part in range(parts):
                for owner in range(samps):
                    grid_sum[part, owner * theta_rows : (owner + 1) * theta_rows] = incoming[chunk][
                        parent, part, owner
                    ]

            def one_child(kid, inner):
                spot = octant[parent, kid]
                real, imag = grid_sum[0], grid_sum[1]
                cos_part = cosines[chunk][spot]
                sin_part = sines[chunk][spot]
                turned = jnp.concatenate(
                    [real * cos_part + imag * sin_part, imag * cos_part - real * sin_part], axis=1
                )
                high, low = split(turned)
                both = dot(theta_down[...], high)
                narrow = both[: 2 * half] + (both[2 * half :] + dot(theta_down[: 2 * half], low))
                for place, piece in enumerate(split(narrow)):
                    for parity in range(2):
                        for part in range(parts):
                            wide_out[
                                parity, kid * parts + part, :, place * LANES : (place + 1) * LANES
                            ] = piece[parity * half : (parity + 1) * half, part * LANES : (part + 1) * LANES]
                return inner

            lax.fori_loop(0, kids, one_child, 0)
            ends = []
            for parity in range(2):
                flat = wide_out[parity].reshape(kids * parts * half, 2 * LANES)
                ends.append(dot(flat, mats[parity][0]) + dot(flat[:, :LANES], mats[parity][1]))
            left, right = ends
            shared = 2 * edge - width
            joined = jnp.concatenate(
                [left[:, : edge - shared], left[:, edge - shared :] + right[:, :shared], right[:, shared:]],
                axis=1,
            ).reshape(kids, parts, half, width)
            for part in range(parts):
                for place in range(per_row):
                    spot = tile(parent, part, place)
                    piece = joined[:, part, :, place * LANES : (place + 1) * LANES]
                    if first:
                        field[spot] = piece
                    else:
                        field[spot] = field[spot] + piece
            return carry

        lax.fori_loop(0, per_device, one_parent, 0)

    def share(chunk, part):
        await_bytes(sources[chunk].at[held_in(group, part)], out_recv.at[chunk, part])
        for bit, held in plan:
            hop(chunk, bit, 0, part).start()

    def pass_on(chunk, part):
        for position, (bit, held) in enumerate(plan):
            for mask in held:
                if mask == 0:
                    continue
                hop(chunk, bit, mask, part).start()
            if position + 1 < len(plan):
                for mask in [h + bit for h in held]:
                    await_bytes(sources[chunk].at[held_in(owner_of(mask), part)], box_recv.at[chunk, hop_slot(mask, part)])

    def back_far_part(chunk, slot):
        def one(step, carry):
            back_part(chunk, slot, (1 - side) * middle + step).start()
            return carry

        @pl.when(outer)
        def _():
            lax.fori_loop(0, middle, one, 0)

    def back_far(chunk):
        def one(slot, carry):
            back_far_part(chunk, slot)
            return carry

        lax.fori_loop(0, per_device, one, 0)

    def translate(chunk, between):
        await_bytes(sources[chunk].at[pl.ds(0, boxes // 2 * samps * per_device)], box_recv.at[chunk, 0])
        load(chunk).wait()

        def receivers(slot, carry):
            if between:

                @pl.when(slot == per_device // 2)
                def _():
                    run(between)

            def one(step, inner):
                peer = lax.rem(me + 1 + step, samps)
                row = (group * samps + peer) * per_device + slot
                real = jnp.zeros(results[chunk].shape[3:], jnp.float32)
                imag = jnp.zeros(results[chunk].shape[3:], jnp.float32)
                for q in range(partners):
                    source = src_rows[q, row]
                    which = disp_rows[q, row]
                    a = sources[chunk][source, 0]
                    b = sources[chunk][source, 1]
                    c = operators[chunk][which, 0]
                    d = operators[chunk][which, 1]
                    real = real + (c * a - d * b)
                    imag = imag + (c * b + d * a)
                results[chunk][peer, slot, 0] = real
                results[chunk][peer, slot, 1] = imag

                there = lax.rem(me + step, samps)

                @pl.when(jnp.logical_and(step > 0, jnp.logical_not(jnp.logical_and(outer, far(there)))))
                def _():
                    back_part(chunk, slot, there).start()

                return inner

            lax.fori_loop(0, samps, one, 0)
            return carry

        lax.fori_loop(0, per_device, receivers, 0)

    def returned_part(chunk, parent):
        await_bytes(incoming[chunk].at[parent, :, pl.ds(0, samps - 1)], back_recv.at[chunk * per_device + parent])

    load_angle(0).start()
    for parent in range(per_device):
        load_child(parent).start()
    for copy in small:
        copy.start()
    load_angle(0).wait()
    turn(0)
    for copy in small:
        copy.wait()
    build_theta()
    for parent in range(per_device):
        load_child(parent).wait()
    for chunk in range(1, chunks):
        load_angle(chunk).start()
    for chunk in range(chunks):
        load(chunk).start()
    called = {(send_far, 0)}

    def fresh(*calls):
        left = [call for call in calls if 0 <= call[1] < chunks and call not in called]
        called.update(left)
        return left

    def run(calls):
        for function, *rest in calls:
            function(*rest)

    aggregate(0, [])
    for chunk in range(1, chunks):
        load_angle(chunk).wait()
        turn(chunk)
        send_last(chunk - 1)
        if chunk > 1:
            run(fresh((send_far, chunk - 1)))
        run(fresh((share, chunk - 2, 1)))
        aggregate(chunk, fresh((share, chunk - 1, 0), (pass_on, chunk - 2, 0)))
    last = chunks - 1
    send_last(last)
    for chunk in range(chunks):
        if chunk == last:
            run(fresh((send_far, last), (pass_on, last, 0), (share, last, 1), (back_far, last - 2)))
        run(fresh((share, chunk, 0), (pass_on, chunk, 0)))
        run(fresh((share, chunk, 1), (pass_on, chunk, 1)))
        if chunk:
            back_keep(chunk - 1).start()
        translate(chunk, fresh((share, chunk + 1, 1), (send_far, last), (share, last, 0)) if chunk + 1 < last else [])
    for chunk in range(last):
        run(fresh((back_far, chunk)))
        if chunk + 1 < last:
            run(fresh((back_far, chunk + 1)))
        back_keep(chunk).wait()
        if chunk == 0:
            back_keep(last).start()
        disaggregate(chunk, chunk == 0, [(back_far_part, last)] if chunk + 1 == last else [])
    if last == 0:
        run(fresh((back_far, last)))
        back_keep(last).start()
    back_keep(last).wait()

    for chunk in range(chunks):
        await_bytes(outgoing[chunk].at[:, :, pl.ds(0, samps - 1)], out_send.at[chunk])
        await_bytes(sources[chunk].at[pl.ds(0, (boxes - 1) * samps * per_device)], box_send.at[chunk])
        if chunk < last:
            await_bytes(results[chunk].at[pl.ds(0, samps - 1)], back_send.at[chunk])
    disaggregate(last, last == 0, [])
    await_bytes(results[last].at[pl.ds(0, samps - 1)], back_send.at[last])


def local(
    boxes,
    samps,
    child_out,
    child_octant,
    theta_index,
    theta_weight,
    phi_index,
    phi_weight,
    shift_angle,
    partner_src,
    partner_disp,
    translation,
):
    child_count, parts, samples = child_out.shape
    parents, kids = child_octant.shape
    octant_count, rows2, cols2 = shift_angle.shape
    partners = partner_src.shape[1]
    theta_rows = rows2 // samps
    chunks = cols2 // LANES
    tiles = samples // LANES
    child = child_out.reshape(child_count, parts, tiles, LANES).transpose(0, 2, 1, 3)
    child = child.reshape(child_count, tiles * parts, LANES)
    block = (parents, parts, theta_rows, LANES)
    spread = (parents, parts, samps, theta_rows, LANES)
    turns = (octant_count, rows2, LANES)
    anywhere = pl.BlockSpec(memory_space=pl.ANY)
    vectors = pl.BlockSpec(memory_space=pltpu.VMEM)
    dma = pltpu.SemaphoreType.DMA

    def per_chunk(shape):
        return [pltpu.VMEM(shape, jnp.float32)] * chunks

    child_in = pl.pallas_call(
        functools.partial(step_kernel, boxes, samps, partners),
        out_shape=pltpu.VMEM(child.shape, jnp.float32),
        in_specs=[anywhere] * 10,
        out_specs=vectors,
        scratch_shapes=[
            pltpu.VMEM((kids, 3 * NT1, parts * LANES), jnp.bfloat16),
            pltpu.VMEM((2, kids * parts, NT1 // 2, 2 * LANES), jnp.bfloat16),
            pltpu.VMEM((parts, rows2, LANES), jnp.float32),
            pltpu.VMEM((rows2, 3 * NT1), jnp.bfloat16),
            pltpu.VMEM((2 * NT1, rows2), jnp.bfloat16),
            pltpu.SMEM(partner_src.shape[::-1], jnp.int32),
            pltpu.SMEM(partner_disp.shape[::-1], jnp.int32),
            pltpu.SMEM(child_octant.shape, jnp.int32),
            pltpu.VMEM(theta_index.shape[::-1], jnp.int32),
            pltpu.VMEM(theta_weight.shape[::-1], jnp.float32),
            pltpu.VMEM(phi_index.shape[::-1], jnp.int32),
            pltpu.VMEM(phi_weight.shape[::-1], jnp.float32),
        ]
        + per_chunk((boxes * samps * parents,) + block[1:])
        + per_chunk(translation.shape[:3] + (LANES,))
        + per_chunk((samps,) + block)
        + per_chunk(spread)
        + per_chunk(spread)
        + per_chunk(turns)
        + per_chunk(turns)
        + [
            dma((parents,)),
            dma((chunks,)),
            dma((chunks,)),
            dma((chunks,)),
            dma((chunks, 2)),
            dma((chunks,)),
            dma((chunks, boxes - 1)),
            dma((chunks,)),
            dma((chunks,)),
            dma((chunks * parents,)),
            dma((7,)),
        ],
        compiler_params=pltpu.CompilerParams(
            collective_id=0, has_side_effects=True, vmem_limit_bytes=VMEM_LIMIT
        ),
    )(
        partner_src.T,
        partner_disp.T,
        child_octant,
        theta_index.T,
        theta_weight.T,
        phi_index.T,
        phi_weight.T,
        child,
        shift_angle,
        translation,
    )
    child_in = child_in.reshape(child_count, tiles, parts, LANES).transpose(0, 2, 1, 3)
    return child_in.reshape(child_count, parts, samples)


def solution(mesh):
    in_specs = (
        P(("box", "samp"), None, None),
        P(("box", "samp"), None),
        P(),
        P(),
        P(),
        P(),
        P(),
        P(),
        P(),
        P(None, None, "samp", None),
    )
    out_specs = P(("box", "samp"), None, None)
    body = functools.partial(local, mesh.shape["box"], mesh.shape["samp"])
    return jax.shard_map(body, mesh=mesh, in_specs=in_specs, out_specs=out_specs, check_vma=False)
```

```python
import functools

import jax
import jax.numpy as jnp
from jax import lax
from jax.experimental import pallas as pl
from jax.experimental.pallas import tpu as pltpu
from jax.sharding import PartitionSpec as P

NT1 = 96
NP1 = 192
LANES = 128
MESH = pl.DeviceIdType.MESH
DELAY = 1
VMEM_LIMIT = 56 * 1024 * 1024


def split(values):
    high = values.astype(jnp.bfloat16)
    low = (values - high.astype(jnp.float32)).astype(jnp.bfloat16)
    return high, low


def dot(left, right):
    return jnp.dot(left, right, preferred_element_type=jnp.float32)


def stencil(wanted, index, weight, axis):
    total = jnp.zeros(wanted.shape, jnp.float32)
    for j in range(index.shape[axis]):
        one = slice(j, j + 1)
        spot = (slice(None), one) if axis == 1 else (one, slice(None))
        total = total + jnp.where(wanted == index[spot], weight[spot], 0.0)
    return total


def iota(shape, axis):
    return lax.broadcasted_iota(jnp.int32, shape, axis)


HALF_PI = (1.5703125, 4.837512969970703e-4, 7.54978995489188e-8)


def cos_sin(angle):
    turns = jnp.floor(angle * 0.6366197723675814 + 0.5)
    rest = ((angle - turns * HALF_PI[0]) - turns * HALF_PI[1]) - turns * HALF_PI[2]
    square = rest * rest
    sine = -1.9515295891e-4 * square + 8.3321608736e-3
    sine = (sine * square - 1.6666654611e-1) * square * rest + rest
    cosine = 2.443315711809948e-5 * square - 1.388731625493765e-3
    cosine = (cosine * square + 4.166664568298827e-2) * square * square - 0.5 * square + 1.0
    half = jnp.floor(turns * 0.5)
    odd = turns - 2.0 * half > 0.5
    flip = half - 2.0 * jnp.floor(half * 0.5) > 0.5
    sin_part = jnp.where(odd, cosine, sine)
    cos_part = jnp.where(odd, -sine, cosine)
    return jnp.where(flip, -cos_part, cos_part), jnp.where(flip, -sin_part, sin_part)


def step_kernel(
    boxes,
    samps,
    partners,
    src_in,
    disp_in,
    octant_in,
    theta_index_in,
    theta_weight_in,
    phi_index_in,
    phi_weight_in,
    child,
    angle,
    table,
    field,
    wide,
    wide_out,
    grid_sum,
    theta_up,
    theta_down,
    src_rows,
    disp_rows,
    octant,
    theta_index_t,
    theta_weight_t,
    phi_index_t,
    phi_weight_t,
    *scratch,
):
    half = NT1 // 2
    width = 2 * NP1
    chunks = angle.shape[2] // LANES
    rows2 = angle.shape[1]
    sources = scratch[:chunks]
    operators = scratch[chunks : 2 * chunks]
    results = scratch[2 * chunks : 3 * chunks]
    outgoing = scratch[3 * chunks : 4 * chunks]
    incoming = scratch[4 * chunks : 5 * chunks]
    cosines = scratch[5 * chunks : 6 * chunks]
    sines = scratch[6 * chunks : 7 * chunks]
    (
        child_sem,
        angle_sem,
        load_sem,
        out_send,
        out_recv,
        box_send,
        box_recv,
        back_own,
        back_send,
        back_recv,
        small_sem,
    ) = scratch[7 * chunks :]
    per_device, parts = outgoing[0].shape[:2]
    kids = child.shape[0] // per_device
    per_row = width // LANES
    theta_rows = rows2 // samps
    edge = -(-(width // 2) // LANES) * LANES
    gap = edge - width // 2
    group = lax.axis_index("box")
    me = lax.axis_index("samp")
    bits = [1 << i for i in range(boxes.bit_length() - 1)][::-1]

    def mate(bit):
        return group + bit - 2 * bit * lax.rem(lax.div(group, bit), 2)

    barrier = pltpu.get_barrier_semaphore()
    for step in range(1, samps):
        pl.semaphore_signal(barrier, inc=1, device_id=(group, lax.rem(me + step, samps)), device_id_type=MESH)
    for bit in bits:
        pl.semaphore_signal(barrier, inc=1, device_id=(mate(bit), me), device_id_type=MESH)

    def load(chunk):
        return pltpu.make_async_copy(
            table.at[:, :, :, pl.ds(chunk * LANES, LANES)], operators[chunk], load_sem.at[chunk]
        )

    def held_by(box, samp):
        return pl.ds((box * samps + samp) * per_device, per_device)

    last = chunks - 1
    middle = max(1, samps // 2)
    side = lax.div(me, middle)
    rim = max(1, samps // 4)

    def at_rim(peer):
        return jnp.logical_or(peer < rim, peer >= samps - rim)

    outer = at_rim(me)

    def apart(peer):
        return lax.rem(lax.div(peer, middle) + side, 2)

    def held_in(box, part):
        start = side if part == 0 else 1 - side
        return pl.ds((box * samps + start * middle) * per_device, middle * per_device)

    def keep(chunk):
        return pltpu.make_async_copy(
            outgoing[chunk].at[:, :, me], sources[chunk].at[held_by(group, me)], out_recv.at[chunk, 0]
        )

    def out_part(chunk, parent, peer):
        return pltpu.make_async_remote_copy(
            src_ref=outgoing[chunk].at[parent, :, peer],
            dst_ref=sources[chunk].at[(group * samps + me) * per_device + parent],
            send_sem=out_send.at[chunk],
            recv_sem=out_recv.at[chunk, apart(peer)],
            device_id=(group, peer),
            device_id_type=MESH,
        )

    def out_copy(chunk, peer):
        return pltpu.make_async_remote_copy(
            src_ref=outgoing[chunk].at[:, :, peer],
            dst_ref=sources[chunk].at[held_by(group, me)],
            send_sem=out_send.at[chunk],
            recv_sem=out_recv.at[chunk, apart(peer)],
            device_id=(group, peer),
            device_id_type=MESH,
        )

    def back_part(chunk, slot, peer):
        return pltpu.make_async_remote_copy(
            src_ref=results[chunk].at[peer, slot],
            dst_ref=incoming[chunk].at[slot, :, me],
            send_sem=back_send.at[chunk],
            recv_sem=back_recv.at[chunk * per_device + slot],
            device_id=(group, peer),
            device_id_type=MESH,
        )

    def await_bytes(ref, sem):
        pltpu.make_async_copy(ref, ref, sem).wait()

    def back_keep(chunk):
        return pltpu.make_async_copy(
            results[chunk].at[me], incoming[chunk].at[:, :, me], back_own.at[chunk]
        )

    def box_plan():
        plan = []
        held = [0]
        for bit in bits:
            plan.append((bit, list(held)))
            held = held + [h + bit for h in held]
        return plan

    plan = box_plan()

    def owner_of(mask):
        spot = group
        for bit in bits:
            if mask & bit:
                spot = spot + bit - 2 * bit * lax.rem(lax.div(group, bit), 2)
        return spot

    def hop_slot(mask, part):
        return 0 if mask % 2 else mask - 1 + part

    def hop(chunk, bit, mask, part):
        spot = held_in(owner_of(mask), part)
        return pltpu.make_async_remote_copy(
            src_ref=sources[chunk].at[spot],
            dst_ref=sources[chunk].at[spot],
            send_sem=box_send.at[chunk],
            recv_sem=box_recv.at[chunk, hop_slot(mask + bit, part)],
            device_id=(mate(bit), me),
            device_id_type=MESH,
        )

    def load_angle(chunk):
        return pltpu.make_async_copy(
            angle.at[:, :, pl.ds(chunk * LANES, LANES)], cosines[chunk], angle_sem.at[chunk]
        )

    small = [
        pltpu.make_async_copy(source, place, small_sem.at[spot])
        for spot, (source, place) in enumerate(
            (
                (octant_in, octant),
                (theta_index_in, theta_index_t),
                (theta_weight_in, theta_weight_t),
                (phi_index_in, phi_index_t),
                (phi_weight_in, phi_weight_t),
                (src_in, src_rows),
                (disp_in, disp_rows),
            )
        )
    ]
    def load_child(parent):
        rows = pl.ds(parent * kids, kids)
        return pltpu.make_async_copy(child.at[rows], field.at[rows], child_sem.at[parent])

    def tile(parent, part, place):
        return (
            pl.ds(parent * kids, kids),
            pl.ds(place * parts + part, half, stride=per_row * parts),
            slice(None),
        )

    def build_theta():
        spot = iota((2 * half, rows2), 0)
        sample = jnp.where(spot < half, 2 * spot, 2 * (spot - half) + 1)
        narrow = stencil(sample, theta_index_t, theta_weight_t, 0)
        high, low = split(narrow.T)
        theta_up[:, : 2 * half] = high
        theta_up[:, 2 * half : 4 * half] = high
        theta_up[:, 4 * half :] = low
        high, low = split(narrow)
        theta_down[: 2 * half] = high
        theta_down[2 * half :] = low

    def turn(chunk):
        def one(spot, carry):
            cos_part, sin_part = cos_sin(cosines[chunk][spot])
            cosines[chunk][spot] = cos_part
            sines[chunk][spot] = sin_part
            return carry

        lax.fori_loop(0, cosines[chunk].shape[0], one, 0)

    def far(peer):
        return lax.div(peer, middle) != side

    def send_out(chunk, parent):
        spot = me - side * middle

        def near_one(step, carry):
            out_part(chunk, parent, side * middle + lax.rem(spot + step, middle)).start()
            return carry

        def far_one(step, carry):
            out_part(chunk, parent, (1 - side) * middle + lax.rem(spot + step, middle)).start()
            return carry

        lax.fori_loop(1, middle, near_one, 0)
        if chunk == 0:
            lax.fori_loop(0, middle, far_one, 0)
        else:

            @pl.when(jnp.logical_not(outer))
            def _():
                lax.fori_loop(0, middle, far_one, 0)

    def send_far(chunk):
        def one(step, carry):
            peer = lax.rem(me + step, samps)

            @pl.when(jnp.logical_and(outer, far(peer)))
            def _():
                out_copy(chunk, peer).start()

            return carry

        lax.fori_loop(1, samps, one, 0)

    def send_last(chunk):
        if chunk > 0:
            send_out(chunk, per_device - 1)
        keep(chunk).start()

    def aggregate(chunk, between):
        lanes = slice(chunk * LANES, (chunk + 1) * LANES)
        sample = iota((edge, LANES), 0)
        mats = []
        for shift in (0, gap):
            high, low = split(stencil(sample - shift, phi_index_t[:, lanes], phi_weight_t[:, lanes], 0))
            mats.append(jnp.concatenate([high, low], axis=1))

        def interpolate(parent):
            if chunk == 0:
                load_child(parent).wait()
            block = jnp.concatenate(
                [
                    jnp.concatenate(
                        [field[tile(parent, part, place)].reshape(kids * half, LANES) for place in range(per_row)],
                        axis=1,
                    )
                    for part in range(parts)
                ],
                axis=0,
            )
            pieces = []
            for mat, start in zip(mats, (0, width - edge)):
                high, low = split(block[:, start : start + edge])
                both = dot(high, mat)
                pieces.append(split(both[:, :LANES] + (both[:, LANES:] + dot(low, mat[:, :LANES]))))
            even, odd = pieces
            for slot, piece in enumerate((even[0], odd[0], even[1], odd[1], even[0], odd[0])):
                piece = piece.reshape(parts, kids, half, LANES)
                for part in range(parts):
                    wide[:, slot * half : (slot + 1) * half, part * LANES : (part + 1) * LANES] = piece[part]

        def first_half(turned, carry):
            part_of = lax.rem(turned + 1 - side, 2)
            rows = pl.ds(pl.multiple_of(part_of * (rows2 // 2), rows2 // 2), rows2 // 2)

            def one_octant(spot, inner):
                kid = 0
                for other in range(1, kids):
                    kid = jnp.where(octant[0, other] == spot, other, kid)
                fine = dot(theta_up[rows], wide[kid])
                real, imag = fine[:, :LANES], fine[:, LANES:]
                cos_part, sin_part = cos_sin(cosines[chunk][spot, rows])
                cosines[chunk][spot, rows] = cos_part
                sines[chunk][spot, rows] = sin_part
                grid_sum[0, rows] += real * cos_part - imag * sin_part
                grid_sum[1, rows] += real * sin_part + imag * cos_part
                return inner

            lax.fori_loop(0, kids, one_octant, 0)
            for owner in range(samps):

                @pl.when(part_of == owner // middle)
                def _():
                    for part in range(parts):
                        outgoing[chunk][0, part, owner] = grid_sum[
                            part, owner * theta_rows : (owner + 1) * theta_rows
                        ]

            @pl.when(turned == 0)
            def _():
                pl.semaphore_wait(barrier, samps - 1 + len(bits))

            def one(step, inner):
                peer = part_of * middle + step

                @pl.when(peer != me)
                def _():
                    out_part(chunk, 0, peer).start()

                return inner

            lax.fori_loop(0, middle, one, 0)
            return carry

        def one_parent(parent, carry):
            interpolate(parent)
            grid_sum[...] = jnp.zeros_like(grid_sum)

            if chunk > 0:

                @pl.when(parent > 0)
                def _():
                    send_out(chunk, parent - 1)

            if between:

                @pl.when(parent == min(1, per_device - 1))
                def _():
                    run(between)

            def one_child(kid, inner):
                spot = octant[parent, kid]
                fine = dot(theta_up[...], wide[kid])
                real, imag = fine[:, :LANES], fine[:, LANES:]
                cos_part = cosines[chunk][spot]
                sin_part = sines[chunk][spot]
                grid_sum[0] += real * cos_part - imag * sin_part
                grid_sum[1] += real * sin_part + imag * cos_part
                return inner

            lax.fori_loop(0, kids, one_child, 0)
            for part in range(parts):
                for owner in range(samps):
                    outgoing[chunk][parent, part, owner] = grid_sum[
                        part, owner * theta_rows : (owner + 1) * theta_rows
                    ]
            if chunk == 0:

                @pl.when(parent == per_device - 1)
                def _():
                    for later in range(chunks):
                        load(later).start()

                send_out(chunk, parent)
            return carry

        if chunk == 0:
            interpolate(0)
            grid_sum[...] = jnp.zeros_like(grid_sum)
            load_angle(chunk).wait()
            lax.fori_loop(0, 2, first_half, 0)
        lax.fori_loop(1 if chunk == 0 else 0, per_device, one_parent, 0)

    def disaggregate(chunk, first, between):
        rows = slice(chunk * LANES, (chunk + 1) * LANES)
        sample = iota((edge, LANES), 0)
        mats = []
        for shift in (0, gap):
            high, low = split(stencil(sample - shift, phi_index_t[:, rows], phi_weight_t[:, rows], 0).T)
            mats.append((jnp.concatenate([high, high], axis=0), low))

        def one_parent(parent, carry):
            returned_part(chunk, parent)
            for function in between:
                function(parent)
            for part in range(parts):
                for owner in range(samps):
                    grid_sum[part, owner * theta_rows : (owner + 1) * theta_rows] = incoming[chunk][
                        parent, part, owner
                    ]

            def one_child(kid, inner):
                spot = octant[parent, kid]
                real, imag = grid_sum[0], grid_sum[1]
                cos_part = cosines[chunk][spot]
                sin_part = sines[chunk][spot]
                turned = jnp.concatenate(
                    [real * cos_part + imag * sin_part, imag * cos_part - real * sin_part], axis=1
                )
                high, low = split(turned)
                both = dot(theta_down[...], high)
                narrow = both[: 2 * half] + (both[2 * half :] + dot(theta_down[: 2 * half], low))
                for place, piece in enumerate(split(narrow)):
                    for parity in range(2):
                        for part in range(parts):
                            wide_out[
                                parity, kid * parts + part, :, place * LANES : (place + 1) * LANES
                            ] = piece[parity * half : (parity + 1) * half, part * LANES : (part + 1) * LANES]
                return inner

            lax.fori_loop(0, kids, one_child, 0)
            ends = []
            for parity in range(2):
                flat = wide_out[parity].reshape(kids * parts * half, 2 * LANES)
                ends.append(dot(flat, mats[parity][0]) + dot(flat[:, :LANES], mats[parity][1]))
            left, right = ends
            shared = 2 * edge - width
            joined = jnp.concatenate(
                [left[:, : edge - shared], left[:, edge - shared :] + right[:, :shared], right[:, shared:]],
                axis=1,
            ).reshape(kids, parts, half, width)
            for part in range(parts):
                for place in range(per_row):
                    spot = tile(parent, part, place)
                    piece = joined[:, part, :, place * LANES : (place + 1) * LANES]
                    if first:
                        field[spot] = piece
                    else:
                        field[spot] = field[spot] + piece
            return carry

        lax.fori_loop(0, per_device, one_parent, 0)

    def share(chunk, part):
        await_bytes(sources[chunk].at[held_in(group, part)], out_recv.at[chunk, part])
        for bit, held in plan:
            hop(chunk, bit, 0, part).start()

    def pass_on(chunk, part):
        for position, (bit, held) in enumerate(plan):
            for mask in held:
                if mask == 0:
                    continue
                hop(chunk, bit, mask, part).start()
            if position + 1 < len(plan):
                for mask in [h + bit for h in held]:
                    await_bytes(sources[chunk].at[held_in(owner_of(mask), part)], box_recv.at[chunk, hop_slot(mask, part)])

    def back_far_part(chunk, slot, wanted=None):
        def one(step, carry):
            peer = (1 - side) * middle + step

            @pl.when(jnp.logical_or(wanted is None, at_rim(peer) == bool(wanted)))
            def _():
                back_part(chunk, slot, peer).start()

            return carry

        lax.fori_loop(0, middle, one, 0)

    def back_far(chunk):
        def one(slot, carry):
            back_far_part(chunk, slot)
            return carry

        @pl.when(outer)
        def _():
            lax.fori_loop(0, per_device, one, 0)

    def back_last(parent):
        def late(slot):
            @pl.when(slot >= 0)
            def _():
                back_far_part(last, slot, False)

        @pl.when(outer)
        def _():
            for lead in range(DELAY):

                @pl.when(parent == 0)
                def _():
                    back_far_part(last, lead, True)

            @pl.when(parent + DELAY < per_device)
            def _():
                back_far_part(last, parent + DELAY, True)

            late(parent - DELAY)

            @pl.when(parent == per_device - 1)
            def _():
                for lag in range(DELAY):
                    late(per_device - DELAY + lag)

    def translate(chunk, between):
        await_bytes(sources[chunk].at[pl.ds(0, boxes // 2 * samps * per_device)], box_recv.at[chunk, 0])
        load(chunk).wait()

        def receivers(slot, carry):
            if between:

                @pl.when(slot == per_device // 2)
                def _():
                    run(between)

            def one(step, inner):
                peer = lax.rem(me + 1 + step, samps)
                row = (group * samps + peer) * per_device + slot
                real = jnp.zeros(results[chunk].shape[3:], jnp.float32)
                imag = jnp.zeros(results[chunk].shape[3:], jnp.float32)
                for q in range(partners):
                    source = src_rows[q, row]
                    which = disp_rows[q, row]
                    a = sources[chunk][source, 0]
                    b = sources[chunk][source, 1]
                    c = operators[chunk][which, 0]
                    d = operators[chunk][which, 1]
                    real = real + (c * a - d * b)
                    imag = imag + (c * b + d * a)
                results[chunk][peer, slot, 0] = real
                results[chunk][peer, slot, 1] = imag

                there = lax.rem(me + step, samps)

                distant = far(there)
                late = jnp.logical_and(distant, jnp.logical_not(at_rim(there))) if chunk == last else False

                @pl.when(jnp.logical_and(step > 0, jnp.logical_not(jnp.logical_or(jnp.logical_and(outer, distant), late))))
                def _():
                    back_part(chunk, slot, there).start()

                if chunk == last:

                    @pl.when(jnp.logical_and(jnp.logical_and(late, slot >= DELAY), jnp.logical_not(outer)))
                    def _():
                        back_part(chunk, slot - DELAY, there).start()

                return inner

            lax.fori_loop(0, samps, one, 0)
            return carry

        lax.fori_loop(0, per_device, receivers, 0)
        if chunk == last:

            @pl.when(jnp.logical_not(outer))
            def _():
                for slot in range(max(0, per_device - DELAY), per_device):
                    back_far_part(chunk, slot, False)

    def returned_part(chunk, parent):
        await_bytes(incoming[chunk].at[parent, :, pl.ds(0, samps - 1)], back_recv.at[chunk * per_device + parent])

    for copy in small:
        copy.start()
    load_child(0).start()
    load_angle(0).start()
    for copy in small:
        copy.wait()
    for parent in range(1, per_device):
        load_child(parent).start()
    for chunk in range(1, chunks):
        load_angle(chunk).start()
    build_theta()
    called = {(send_far, 0)}

    def fresh(*calls):
        left = [call for call in calls if 0 <= call[1] < chunks and call not in called]
        called.update(left)
        return left

    def run(calls):
        for function, *rest in calls:
            function(*rest)

    aggregate(0, [])
    for chunk in range(1, chunks):
        load_angle(chunk).wait()
        turn(chunk)
        send_last(chunk - 1)
        if chunk > 1:
            run(fresh((send_far, chunk - 1)))
        run(fresh((share, chunk - 2, 1)))
        aggregate(chunk, fresh((share, chunk - 1, 0), (pass_on, chunk - 2, 0)))
    send_last(last)
    for chunk in range(chunks):
        if chunk == last:
            run(fresh((send_far, last), (share, last, 0), (share, last, 1), (back_far, last - 2), (pass_on, last, 0)))
        run(fresh((share, chunk, 0), (pass_on, chunk, 0)))
        run(fresh((share, chunk, 1), (pass_on, chunk, 1)))
        if chunk:
            run(fresh((share, chunk + 1, 0)))
        if chunk:
            back_keep(chunk - 1).start()
        translate(chunk, fresh((share, chunk + 1, 1), (send_far, last)) if chunk + 1 < last else [])
    for chunk in range(last):
        run(fresh((back_far, chunk)))
        if chunk + 1 < last:
            run(fresh((back_far, chunk + 1)))
        back_keep(chunk).wait()
        if chunk == 0:
            back_keep(last).start()
        disaggregate(chunk, chunk == 0, [back_last] if chunk + 1 == last else [])
    if last == 0:
        run(fresh((back_far, last)))
        back_keep(last).start()
    back_keep(last).wait()

    for chunk in range(chunks):
        await_bytes(outgoing[chunk].at[:, :, pl.ds(0, samps - 1)], out_send.at[chunk])
        await_bytes(sources[chunk].at[pl.ds(0, (boxes - 1) * samps * per_device)], box_send.at[chunk])
        if chunk < last:
            await_bytes(results[chunk].at[pl.ds(0, samps - 1)], back_send.at[chunk])
    disaggregate(last, last == 0, [])
    await_bytes(results[last].at[pl.ds(0, samps - 1)], back_send.at[last])


def local(
    boxes,
    samps,
    child_out,
    child_octant,
    theta_index,
    theta_weight,
    phi_index,
    phi_weight,
    shift_angle,
    partner_src,
    partner_disp,
    translation,
):
    child_count, parts, samples = child_out.shape
    parents, kids = child_octant.shape
    octant_count, rows2, cols2 = shift_angle.shape
    partners = partner_src.shape[1]
    theta_rows = rows2 // samps
    chunks = cols2 // LANES
    tiles = samples // LANES
    child = child_out.reshape(child_count, parts, tiles, LANES).transpose(0, 2, 1, 3)
    child = child.reshape(child_count, tiles * parts, LANES)
    block = (parents, parts, theta_rows, LANES)
    spread = (parents, parts, samps, theta_rows, LANES)
    turns = (octant_count, rows2, LANES)
    anywhere = pl.BlockSpec(memory_space=pl.ANY)
    vectors = pl.BlockSpec(memory_space=pltpu.VMEM)
    dma = pltpu.SemaphoreType.DMA

    def per_chunk(shape):
        return [pltpu.VMEM(shape, jnp.float32)] * chunks

    child_in = pl.pallas_call(
        functools.partial(step_kernel, boxes, samps, partners),
        out_shape=pltpu.VMEM(child.shape, jnp.float32),
        in_specs=[anywhere] * 10,
        out_specs=vectors,
        scratch_shapes=[
            pltpu.VMEM((kids, 3 * NT1, parts * LANES), jnp.bfloat16),
            pltpu.VMEM((2, kids * parts, NT1 // 2, 2 * LANES), jnp.bfloat16),
            pltpu.VMEM((parts, rows2, LANES), jnp.float32),
            pltpu.VMEM((rows2, 3 * NT1), jnp.bfloat16),
            pltpu.VMEM((2 * NT1, rows2), jnp.bfloat16),
            pltpu.SMEM(partner_src.shape[::-1], jnp.int32),
            pltpu.SMEM(partner_disp.shape[::-1], jnp.int32),
            pltpu.SMEM(child_octant.shape, jnp.int32),
            pltpu.VMEM(theta_index.shape[::-1], jnp.int32),
            pltpu.VMEM(theta_weight.shape[::-1], jnp.float32),
            pltpu.VMEM(phi_index.shape[::-1], jnp.int32),
            pltpu.VMEM(phi_weight.shape[::-1], jnp.float32),
        ]
        + per_chunk((boxes * samps * parents,) + block[1:])
        + per_chunk(translation.shape[:3] + (LANES,))
        + per_chunk((samps,) + block)
        + per_chunk(spread)
        + per_chunk(spread)
        + per_chunk(turns)
        + per_chunk(turns)
        + [
            dma((parents,)),
            dma((chunks,)),
            dma((chunks,)),
            dma((chunks,)),
            dma((chunks, 2)),
            dma((chunks,)),
            dma((chunks, boxes - 1)),
            dma((chunks,)),
            dma((chunks,)),
            dma((chunks * parents,)),
            dma((7,)),
        ],
        compiler_params=pltpu.CompilerParams(
            collective_id=0, has_side_effects=True, vmem_limit_bytes=VMEM_LIMIT
        ),
    )(
        partner_src.T,
        partner_disp.T,
        child_octant,
        theta_index.T,
        theta_weight.T,
        phi_index.T,
        phi_weight.T,
        child,
        shift_angle,
        translation,
    )
    child_in = child_in.reshape(child_count, tiles, parts, LANES).transpose(0, 2, 1, 3)
    return child_in.reshape(child_count, parts, samples)


def solution(mesh):
    in_specs = (
        P(("box", "samp"), None, None),
        P(("box", "samp"), None),
        P(),
        P(),
        P(),
        P(),
        P(),
        P(),
        P(),
        P(None, None, "samp", None),
    )
    out_specs = P(("box", "samp"), None, None)
    body = functools.partial(local, mesh.shape["box"], mesh.shape["samp"])
    return jax.shard_map(body, mesh=mesh, in_specs=in_specs, out_specs=out_specs, check_vma=False)
```

```python
import functools

import jax
import jax.numpy as jnp
from jax import lax
from jax.experimental import pallas as pl
from jax.experimental.pallas import tpu as pltpu
from jax.sharding import PartitionSpec as P

NT1 = 96
NP1 = 192
LANES = 128
MESH = pl.DeviceIdType.MESH
DELAY = 1
VMEM_LIMIT = 56 * 1024 * 1024


def split(values):
    high = values.astype(jnp.bfloat16)
    low = (values - high.astype(jnp.float32)).astype(jnp.bfloat16)
    return high, low


def dot(left, right):
    return jnp.dot(left, right, preferred_element_type=jnp.float32)


def stencil(wanted, index, weight, axis):
    total = jnp.zeros(wanted.shape, jnp.float32)
    for j in range(index.shape[axis]):
        one = slice(j, j + 1)
        spot = (slice(None), one) if axis == 1 else (one, slice(None))
        total = total + jnp.where(wanted == index[spot], weight[spot], 0.0)
    return total


def iota(shape, axis):
    return lax.broadcasted_iota(jnp.int32, shape, axis)


HALF_PI = (1.5703125, 4.837512969970703e-4, 7.54978995489188e-8)


def cos_sin(angle):
    turns = jnp.floor(angle * 0.6366197723675814 + 0.5)
    rest = ((angle - turns * HALF_PI[0]) - turns * HALF_PI[1]) - turns * HALF_PI[2]
    square = rest * rest
    sine = -1.9515295891e-4 * square + 8.3321608736e-3
    sine = (sine * square - 1.6666654611e-1) * square * rest + rest
    cosine = 2.443315711809948e-5 * square - 1.388731625493765e-3
    cosine = (cosine * square + 4.166664568298827e-2) * square * square - 0.5 * square + 1.0
    half = jnp.floor(turns * 0.5)
    odd = turns - 2.0 * half > 0.5
    flip = half - 2.0 * jnp.floor(half * 0.5) > 0.5
    sin_part = jnp.where(odd, cosine, sine)
    cos_part = jnp.where(odd, -sine, cosine)
    return jnp.where(flip, -cos_part, cos_part), jnp.where(flip, -sin_part, sin_part)


def step_kernel(
    boxes,
    samps,
    partners,
    src_in,
    disp_in,
    octant_in,
    theta_index_in,
    theta_weight_in,
    phi_index_in,
    phi_weight_in,
    child,
    angle,
    table,
    field,
    wide,
    wide_out,
    grid_sum,
    theta_up,
    theta_down,
    src_rows,
    disp_rows,
    octant,
    theta_index_t,
    theta_weight_t,
    phi_index_t,
    phi_weight_t,
    *scratch,
):
    half = NT1 // 2
    width = 2 * NP1
    chunks = angle.shape[2] // LANES
    rows2 = angle.shape[1]
    sources = scratch[:chunks]
    operators = scratch[chunks : 2 * chunks]
    results = scratch[2 * chunks : 3 * chunks]
    outgoing = scratch[3 * chunks : 4 * chunks]
    incoming = scratch[4 * chunks : 5 * chunks]
    cosines = scratch[5 * chunks : 6 * chunks]
    sines = scratch[6 * chunks : 7 * chunks]
    (
        child_sem,
        angle_sem,
        load_sem,
        out_send,
        out_recv,
        box_send,
        box_recv,
        back_own,
        back_send,
        back_recv,
        small_sem,
    ) = scratch[7 * chunks :]
    per_device, parts = outgoing[0].shape[:2]
    kids = child.shape[0] // per_device
    per_row = width // LANES
    theta_rows = rows2 // samps
    edge = -(-(width // 2) // LANES) * LANES
    gap = edge - width // 2
    group = lax.axis_index("box")
    me = lax.axis_index("samp")
    bits = [1 << i for i in range(boxes.bit_length() - 1)][::-1]

    def mate(bit):
        return group + bit - 2 * bit * lax.rem(lax.div(group, bit), 2)

    def load(chunk):
        return pltpu.make_async_copy(
            table.at[:, :, :, pl.ds(chunk * LANES, LANES)], operators[chunk], load_sem.at[chunk]
        )

    def held_by(box, samp):
        return pl.ds((box * samps + samp) * per_device, per_device)

    last = chunks - 1
    middle = max(1, samps // 2)
    side = lax.div(me, middle)
    rim = max(1, samps // 4)

    def at_rim(peer):
        return jnp.logical_or(peer < rim, peer >= samps - rim)

    outer = at_rim(me)

    def apart(peer):
        return lax.rem(lax.div(peer, middle) + side, 2)

    def held_in(box, part):
        start = side if part == 0 else 1 - side
        return pl.ds((box * samps + start * middle) * per_device, middle * per_device)

    def keep(chunk):
        return pltpu.make_async_copy(
            outgoing[chunk].at[:, :, me], sources[chunk].at[held_by(group, me)], out_recv.at[chunk, 0]
        )

    def out_part(chunk, parent, peer):
        return pltpu.make_async_remote_copy(
            src_ref=outgoing[chunk].at[parent, :, peer],
            dst_ref=sources[chunk].at[(group * samps + me) * per_device + parent],
            send_sem=out_send.at[chunk],
            recv_sem=out_recv.at[chunk, apart(peer)],
            device_id=(group, peer),
            device_id_type=MESH,
        )

    def out_copy(chunk, peer):
        return pltpu.make_async_remote_copy(
            src_ref=outgoing[chunk].at[:, :, peer],
            dst_ref=sources[chunk].at[held_by(group, me)],
            send_sem=out_send.at[chunk],
            recv_sem=out_recv.at[chunk, apart(peer)],
            device_id=(group, peer),
            device_id_type=MESH,
        )

    def back_part(chunk, slot, peer):
        return pltpu.make_async_remote_copy(
            src_ref=results[chunk].at[peer, slot],
            dst_ref=incoming[chunk].at[slot, :, me],
            send_sem=back_send.at[chunk],
            recv_sem=back_recv.at[chunk * per_device + slot],
            device_id=(group, peer),
            device_id_type=MESH,
        )

    def await_bytes(ref, sem):
        pltpu.make_async_copy(ref, ref, sem).wait()

    def back_keep(chunk):
        return pltpu.make_async_copy(
            results[chunk].at[me], incoming[chunk].at[:, :, me], back_own.at[chunk]
        )

    def box_plan():
        plan = []
        held = [0]
        for bit in bits:
            plan.append((bit, list(held)))
            held = held + [h + bit for h in held]
        return plan

    plan = box_plan()

    def owner_of(mask):
        spot = group
        for bit in bits:
            if mask & bit:
                spot = spot + bit - 2 * bit * lax.rem(lax.div(group, bit), 2)
        return spot

    def hop_slot(mask, part):
        return 0 if mask % 2 else mask - 1 + part

    def hop(chunk, bit, mask, part):
        spot = held_in(owner_of(mask), part)
        return pltpu.make_async_remote_copy(
            src_ref=sources[chunk].at[spot],
            dst_ref=sources[chunk].at[spot],
            send_sem=box_send.at[chunk],
            recv_sem=box_recv.at[chunk, hop_slot(mask + bit, part)],
            device_id=(mate(bit), me),
            device_id_type=MESH,
        )

    def load_angle(chunk):
        return pltpu.make_async_copy(
            angle.at[:, :, pl.ds(chunk * LANES, LANES)], cosines[chunk], angle_sem.at[chunk]
        )

    small = [
        pltpu.make_async_copy(source, place, small_sem.at[spot])
        for spot, (source, place) in enumerate(
            (
                (theta_index_in, theta_index_t),
                (theta_weight_in, theta_weight_t),
                (phi_index_in, phi_index_t),
                (phi_weight_in, phi_weight_t),
                (octant_in, octant),
                (src_in, src_rows),
                (disp_in, disp_rows),
            )
        )
    ]
    def load_child(parent):
        rows = pl.ds(parent * kids, kids)
        return pltpu.make_async_copy(child.at[rows], field.at[rows], child_sem.at[parent])

    def tile(parent, part, place):
        return (
            pl.ds(parent * kids, kids),
            pl.ds(place * parts + part, half, stride=per_row * parts),
            slice(None),
        )

    def build_theta():
        spot = iota((2 * half, rows2), 0)
        sample = jnp.where(spot < half, 2 * spot, 2 * (spot - half) + 1)
        narrow = stencil(sample, theta_index_t, theta_weight_t, 0)
        high, low = split(narrow.T)
        theta_up[:, : 2 * half] = high
        theta_up[:, 2 * half : 4 * half] = high
        theta_up[:, 4 * half :] = low
        high, low = split(narrow)
        theta_down[: 2 * half] = high
        theta_down[2 * half :] = low

    def turn(chunk):
        def one(spot, carry):
            cos_part, sin_part = cos_sin(cosines[chunk][spot])
            cosines[chunk][spot] = cos_part
            sines[chunk][spot] = sin_part
            return carry

        lax.fori_loop(0, cosines[chunk].shape[0], one, 0)

    def far(peer):
        return lax.div(peer, middle) != side

    def send_out(chunk, parent):
        spot = me - side * middle

        def near_one(step, carry):
            out_part(chunk, parent, side * middle + lax.rem(spot + step, middle)).start()
            return carry

        def far_one(step, carry):
            out_part(chunk, parent, (1 - side) * middle + lax.rem(spot + step, middle)).start()
            return carry

        lax.fori_loop(1, middle, near_one, 0)
        if chunk == 0:
            lax.fori_loop(0, middle, far_one, 0)
        else:

            @pl.when(jnp.logical_not(outer))
            def _():
                lax.fori_loop(0, middle, far_one, 0)

    def send_far(chunk):
        def one(step, carry):
            peer = lax.rem(me + step, samps)

            @pl.when(jnp.logical_and(outer, far(peer)))
            def _():
                out_copy(chunk, peer).start()

            return carry

        lax.fori_loop(1, samps, one, 0)

    def send_last(chunk):
        if chunk > 0:
            send_out(chunk, per_device - 1)
        keep(chunk).start()

    def aggregate(chunk, between):
        lanes = slice(chunk * LANES, (chunk + 1) * LANES)
        sample = iota((edge, LANES), 0)
        mats = []
        for shift in (0, gap):
            high, low = split(stencil(sample - shift, phi_index_t[:, lanes], phi_weight_t[:, lanes], 0))
            mats.append(jnp.concatenate([high, low], axis=1))

        def interpolate(parent):
            if chunk == 0:
                load_child(parent).wait()
            block = jnp.concatenate(
                [
                    jnp.concatenate(
                        [field[tile(parent, part, place)].reshape(kids * half, LANES) for place in range(per_row)],
                        axis=1,
                    )
                    for part in range(parts)
                ],
                axis=0,
            )
            pieces = []
            for mat, start in zip(mats, (0, width - edge)):
                high, low = split(block[:, start : start + edge])
                both = dot(high, mat)
                pieces.append(split(both[:, :LANES] + (both[:, LANES:] + dot(low, mat[:, :LANES]))))
            even, odd = pieces
            for slot, piece in enumerate((even[0], odd[0], even[1], odd[1], even[0], odd[0])):
                piece = piece.reshape(parts, kids, half, LANES)
                for part in range(parts):
                    wide[:, slot * half : (slot + 1) * half, part * LANES : (part + 1) * LANES] = piece[part]

        def first_half(turned, carry):
            part_of = lax.rem(turned + 1 - side, 2)
            rows = pl.ds(pl.multiple_of(part_of * (rows2 // 2), rows2 // 2), rows2 // 2)

            def one_octant(spot, inner):
                kid = 0
                for other in range(1, kids):
                    kid = jnp.where(octant[0, other] == spot, other, kid)
                fine = dot(theta_up[rows], wide[kid])
                real, imag = fine[:, :LANES], fine[:, LANES:]
                cos_part, sin_part = cos_sin(cosines[chunk][spot, rows])
                cosines[chunk][spot, rows] = cos_part
                sines[chunk][spot, rows] = sin_part
                grid_sum[0, rows] += real * cos_part - imag * sin_part
                grid_sum[1, rows] += real * sin_part + imag * cos_part
                return inner

            lax.fori_loop(0, kids, one_octant, 0, unroll=8)
            for owner in range(samps):

                @pl.when(part_of == owner // middle)
                def _():
                    for part in range(parts):
                        outgoing[chunk][0, part, owner] = grid_sum[
                            part, owner * theta_rows : (owner + 1) * theta_rows
                        ]

            @pl.when(turned == 0)
            def _():
                pl.semaphore_wait(barrier, samps - 1 + len(bits))

            def one(step, inner):
                peer = part_of * middle + step

                @pl.when(peer != me)
                def _():
                    out_part(chunk, 0, peer).start()

                return inner

            lax.fori_loop(0, middle, one, 0)
            return carry

        def one_parent(parent, carry):
            interpolate(parent)
            grid_sum[...] = jnp.zeros_like(grid_sum)

            if chunk > 0:

                @pl.when(parent > 0)
                def _():
                    send_out(chunk, parent - 1)

            if between:

                @pl.when(parent == per_device // 2)
                def _():
                    run(between)

            def one_child(kid, inner):
                spot = octant[parent, kid]
                fine = dot(theta_up[...], wide[kid])
                real, imag = fine[:, :LANES], fine[:, LANES:]
                cos_part = cosines[chunk][spot]
                sin_part = sines[chunk][spot]
                grid_sum[0] += real * cos_part - imag * sin_part
                grid_sum[1] += real * sin_part + imag * cos_part
                return inner

            lax.fori_loop(0, kids, one_child, 0, unroll=8)
            for part in range(parts):
                for owner in range(samps):
                    outgoing[chunk][parent, part, owner] = grid_sum[
                        part, owner * theta_rows : (owner + 1) * theta_rows
                    ]
            if chunk == 0:

                @pl.when(parent == per_device - 1)
                def _():
                    for later in range(chunks):
                        load(later).start()

                send_out(chunk, parent)
            return carry

        if chunk == 0:
            interpolate(0)
            grid_sum[...] = jnp.zeros_like(grid_sum)
            load_angle(chunk).wait()
            lax.fori_loop(0, 2, first_half, 0)
        lax.fori_loop(1 if chunk == 0 else 0, per_device, one_parent, 0)

    def disaggregate(chunk, first, between):
        rows = slice(chunk * LANES, (chunk + 1) * LANES)
        sample = iota((edge, LANES), 0)
        mats = []
        for shift in (0, gap):
            high, low = split(stencil(sample - shift, phi_index_t[:, rows], phi_weight_t[:, rows], 0).T)
            mats.append((jnp.concatenate([high, high], axis=0), low))

        def one_parent(parent, carry):
            returned_part(chunk, parent)
            for function in between:
                function(parent)
            for part in range(parts):
                for owner in range(samps):
                    grid_sum[part, owner * theta_rows : (owner + 1) * theta_rows] = incoming[chunk][
                        parent, part, owner
                    ]

            def one_child(kid, inner):
                spot = octant[parent, kid]
                real, imag = grid_sum[0], grid_sum[1]
                cos_part = cosines[chunk][spot]
                sin_part = sines[chunk][spot]
                turned = jnp.concatenate(
                    [real * cos_part + imag * sin_part, imag * cos_part - real * sin_part], axis=1
                )
                high, low = split(turned)
                both = dot(theta_down[...], high)
                narrow = both[: 2 * half] + (both[2 * half :] + dot(theta_down[: 2 * half], low))
                for place, piece in enumerate(split(narrow)):
                    for parity in range(2):
                        for part in range(parts):
                            wide_out[
                                parity, kid * parts + part, :, place * LANES : (place + 1) * LANES
                            ] = piece[parity * half : (parity + 1) * half, part * LANES : (part + 1) * LANES]
                return inner

            lax.fori_loop(0, kids, one_child, 0, unroll=8)
            ends = []
            for parity in range(2):
                flat = wide_out[parity].reshape(kids * parts * half, 2 * LANES)
                ends.append(dot(flat, mats[parity][0]) + dot(flat[:, :LANES], mats[parity][1]))
            left, right = ends
            shared = 2 * edge - width
            joined = jnp.concatenate(
                [left[:, : edge - shared], left[:, edge - shared :] + right[:, :shared], right[:, shared:]],
                axis=1,
            ).reshape(kids, parts, half, width)
            for part in range(parts):
                for place in range(per_row):
                    spot = tile(parent, part, place)
                    piece = joined[:, part, :, place * LANES : (place + 1) * LANES]
                    if first:
                        field[spot] = piece
                    else:
                        field[spot] = field[spot] + piece
            return carry

        lax.fori_loop(0, per_device, one_parent, 0)

    def share(chunk, part):
        await_bytes(sources[chunk].at[held_in(group, part)], out_recv.at[chunk, part])
        for bit, held in plan:
            hop(chunk, bit, 0, part).start()

    def pass_on(chunk, part):
        for position, (bit, held) in enumerate(plan):
            for mask in held:
                if mask == 0:
                    continue
                hop(chunk, bit, mask, part).start()
            if position + 1 < len(plan):
                for mask in [h + bit for h in held]:
                    await_bytes(sources[chunk].at[held_in(owner_of(mask), part)], box_recv.at[chunk, hop_slot(mask, part)])

    def back_far_part(chunk, slot, wanted=None):
        def one(step, carry):
            peer = (1 - side) * middle + step

            @pl.when(jnp.logical_or(wanted is None, at_rim(peer) == bool(wanted)))
            def _():
                back_part(chunk, slot, peer).start()

            return carry

        lax.fori_loop(0, middle, one, 0)

    def back_far(chunk):
        def one(slot, carry):
            back_far_part(chunk, slot)
            return carry

        @pl.when(outer)
        def _():
            lax.fori_loop(0, per_device, one, 0)

    def back_last(parent):
        def late(slot):
            @pl.when(slot >= 0)
            def _():
                back_far_part(last, slot, False)

        @pl.when(outer)
        def _():
            for lead in range(DELAY):

                @pl.when(parent == 0)
                def _():
                    back_far_part(last, lead, True)

            @pl.when(parent + DELAY < per_device)
            def _():
                back_far_part(last, parent + DELAY, True)

            late(parent - DELAY)

            @pl.when(parent == per_device - 1)
            def _():
                for lag in range(DELAY):
                    late(per_device - DELAY + lag)

    def translate(chunk, between):
        await_bytes(sources[chunk].at[pl.ds(0, boxes // 2 * samps * per_device)], box_recv.at[chunk, 0])
        load(chunk).wait()

        def receivers(slot, carry):
            if between:

                @pl.when(slot == per_device // 2)
                def _():
                    run(between)

            def one(step, inner):
                peer = lax.rem(me + 1 + step, samps)
                row = (group * samps + peer) * per_device + slot
                real = jnp.zeros(results[chunk].shape[3:], jnp.float32)
                imag = jnp.zeros(results[chunk].shape[3:], jnp.float32)
                for q in range(partners):
                    source = src_rows[q, row]
                    which = disp_rows[q, row]
                    a = sources[chunk][source, 0]
                    b = sources[chunk][source, 1]
                    c = operators[chunk][which, 0]
                    d = operators[chunk][which, 1]
                    real = real + (c * a - d * b)
                    imag = imag + (c * b + d * a)
                results[chunk][peer, slot, 0] = real
                results[chunk][peer, slot, 1] = imag

                there = lax.rem(me + step, samps)

                distant = far(there)
                late = jnp.logical_and(distant, jnp.logical_not(at_rim(there))) if chunk == last else False

                @pl.when(jnp.logical_and(step > 0, jnp.logical_not(jnp.logical_or(jnp.logical_and(outer, distant), late))))
                def _():
                    back_part(chunk, slot, there).start()

                if chunk == last:

                    @pl.when(jnp.logical_and(jnp.logical_and(late, slot >= DELAY), jnp.logical_not(outer)))
                    def _():
                        back_part(chunk, slot - DELAY, there).start()

                return inner

            lax.fori_loop(0, samps, one, 0)
            return carry

        lax.fori_loop(0, per_device, receivers, 0)
        if chunk == last:

            @pl.when(jnp.logical_not(outer))
            def _():
                for slot in range(max(0, per_device - DELAY), per_device):
                    back_far_part(chunk, slot, False)

    def returned_part(chunk, parent):
        await_bytes(incoming[chunk].at[parent, :, pl.ds(0, samps - 1)], back_recv.at[chunk * per_device + parent])

    for copy in small[:5]:
        copy.start()
    load_child(0).start()
    load_angle(0).start()
    barrier = pltpu.get_barrier_semaphore()
    for step in range(1, samps):
        pl.semaphore_signal(barrier, inc=1, device_id=(group, lax.rem(me + step, samps)), device_id_type=MESH)
    for bit in bits:
        pl.semaphore_signal(barrier, inc=1, device_id=(mate(bit), me), device_id_type=MESH)
    for copy in small[5:]:
        copy.start()
    for copy in small[:5]:
        copy.wait()
    for parent in range(1, per_device):
        load_child(parent).start()
    for chunk in range(1, chunks):
        load_angle(chunk).start()
    build_theta()
    called = {(send_far, 0)}

    def fresh(*calls):
        left = [call for call in calls if 0 <= call[1] < chunks and call not in called]
        called.update(left)
        return left

    def run(calls):
        for function, *rest in calls:
            function(*rest)

    aggregate(0, [])
    for chunk in range(1, chunks):
        load_angle(chunk).wait()
        turn(chunk)
        send_last(chunk - 1)
        run(fresh((share, chunk - 2, 1)))
        if chunk > 1:
            run(fresh((send_far, chunk - 1)))
        aggregate(chunk, fresh((share, chunk - 1, 0), (pass_on, chunk - 2, 0)))
    send_last(last)
    for copy in small[5:]:
        copy.wait()
    for chunk in range(chunks):
        if chunk == last:
            run(fresh((send_far, last), (share, last, 0), (share, last, 1), (back_far, last - 2), (pass_on, last, 0)))
        run(fresh((share, chunk, 0), (pass_on, chunk, 0)))
        run(fresh((share, chunk, 1), (pass_on, chunk, 1)))
        if chunk:
            run(fresh((share, chunk + 1, 0)))
        if chunk:
            back_keep(chunk - 1).start()
        translate(chunk, fresh((share, chunk + 1, 1), (send_far, last)) if chunk + 1 < last else [])
    for chunk in range(last):
        run(fresh((back_far, chunk)))
        if chunk + 1 < last:
            run(fresh((back_far, chunk + 1)))
        back_keep(chunk).wait()
        if chunk == 0:
            back_keep(last).start()
        disaggregate(chunk, chunk == 0, [back_last] if chunk + 1 == last else [])
    if last == 0:
        run(fresh((back_far, last)))
        back_keep(last).start()
    back_keep(last).wait()

    for chunk in range(chunks):
        await_bytes(outgoing[chunk].at[:, :, pl.ds(0, samps - 1)], out_send.at[chunk])
        await_bytes(sources[chunk].at[pl.ds(0, (boxes - 1) * samps * per_device)], box_send.at[chunk])
        if chunk < last:
            await_bytes(results[chunk].at[pl.ds(0, samps - 1)], back_send.at[chunk])
    disaggregate(last, last == 0, [])
    await_bytes(results[last].at[pl.ds(0, samps - 1)], back_send.at[last])


def local(
    boxes,
    samps,
    child_out,
    child_octant,
    theta_index,
    theta_weight,
    phi_index,
    phi_weight,
    shift_angle,
    partner_src,
    partner_disp,
    translation,
):
    child_count, parts, samples = child_out.shape
    parents, kids = child_octant.shape
    octant_count, rows2, cols2 = shift_angle.shape
    partners = partner_src.shape[1]
    theta_rows = rows2 // samps
    chunks = cols2 // LANES
    tiles = samples // LANES
    child = child_out.reshape(child_count, parts, tiles, LANES).transpose(0, 2, 1, 3)
    child = child.reshape(child_count, tiles * parts, LANES)
    block = (parents, parts, theta_rows, LANES)
    spread = (parents, parts, samps, theta_rows, LANES)
    turns = (octant_count, rows2, LANES)
    anywhere = pl.BlockSpec(memory_space=pl.ANY)
    vectors = pl.BlockSpec(memory_space=pltpu.VMEM)
    dma = pltpu.SemaphoreType.DMA

    def per_chunk(shape):
        return [pltpu.VMEM(shape, jnp.float32)] * chunks

    child_in = pl.pallas_call(
        functools.partial(step_kernel, boxes, samps, partners),
        out_shape=pltpu.VMEM(child.shape, jnp.float32),
        in_specs=[anywhere] * 10,
        out_specs=vectors,
        scratch_shapes=[
            pltpu.VMEM((kids, 3 * NT1, parts * LANES), jnp.bfloat16),
            pltpu.VMEM((2, kids * parts, NT1 // 2, 2 * LANES), jnp.bfloat16),
            pltpu.VMEM((parts, rows2, LANES), jnp.float32),
            pltpu.VMEM((rows2, 3 * NT1), jnp.bfloat16),
            pltpu.VMEM((2 * NT1, rows2), jnp.bfloat16),
            pltpu.SMEM(partner_src.shape[::-1], jnp.int32),
            pltpu.SMEM(partner_disp.shape[::-1], jnp.int32),
            pltpu.SMEM(child_octant.shape, jnp.int32),
            pltpu.VMEM(theta_index.shape[::-1], jnp.int32),
            pltpu.VMEM(theta_weight.shape[::-1], jnp.float32),
            pltpu.VMEM(phi_index.shape[::-1], jnp.int32),
            pltpu.VMEM(phi_weight.shape[::-1], jnp.float32),
        ]
        + per_chunk((boxes * samps * parents,) + block[1:])
        + per_chunk(translation.shape[:3] + (LANES,))
        + per_chunk((samps,) + block)
        + per_chunk(spread)
        + per_chunk(spread)
        + per_chunk(turns)
        + per_chunk(turns)
        + [
            dma((parents,)),
            dma((chunks,)),
            dma((chunks,)),
            dma((chunks,)),
            dma((chunks, 2)),
            dma((chunks,)),
            dma((chunks, boxes - 1)),
            dma((chunks,)),
            dma((chunks,)),
            dma((chunks * parents,)),
            dma((7,)),
        ],
        compiler_params=pltpu.CompilerParams(
            collective_id=0, has_side_effects=True, vmem_limit_bytes=VMEM_LIMIT
        ),
    )(
        partner_src.T,
        partner_disp.T,
        child_octant,
        theta_index.T,
        theta_weight.T,
        phi_index.T,
        phi_weight.T,
        child,
        shift_angle,
        translation,
    )
    child_in = child_in.reshape(child_count, tiles, parts, LANES).transpose(0, 2, 1, 3)
    return child_in.reshape(child_count, parts, samples)


def solution(mesh):
    in_specs = (
        P(("box", "samp"), None, None),
        P(("box", "samp"), None),
        P(),
        P(),
        P(),
        P(),
        P(),
        P(),
        P(),
        P(None, None, "samp", None),
    )
    out_specs = P(("box", "samp"), None, None)
    body = functools.partial(local, mesh.shape["box"], mesh.shape["samp"])
    return jax.shard_map(body, mesh=mesh, in_specs=in_specs, out_specs=out_specs, check_vma=False)
```

```python
import functools

import jax
import jax.numpy as jnp
from jax import lax
from jax.experimental import pallas as pl
from jax.experimental.pallas import tpu as pltpu
from jax.sharding import PartitionSpec as P

NT1 = 96
NP1 = 192
LANES = 128
MESH = pl.DeviceIdType.MESH
OUTER_LAG = 1
INNER_LAG = 2
VMEM_LIMIT = 56 * 1024 * 1024


def split(values):
    high = values.astype(jnp.bfloat16)
    low = (values - high.astype(jnp.float32)).astype(jnp.bfloat16)
    return high, low


def dot(left, right):
    return jnp.dot(left, right, preferred_element_type=jnp.float32)


def stencil(wanted, index, weight, axis):
    total = jnp.zeros(wanted.shape, jnp.float32)
    for j in range(index.shape[axis]):
        one = slice(j, j + 1)
        spot = (slice(None), one) if axis == 1 else (one, slice(None))
        total = total + jnp.where(wanted == index[spot], weight[spot], 0.0)
    return total


def iota(shape, axis):
    return lax.broadcasted_iota(jnp.int32, shape, axis)


HALF_SINE = (0.5, -0.02083333395421505, 0.00026041659293696284, -1.5500672816415317e-06, 5.376032508053186e-09, -1.1664790661169988e-11)
HALF_COSINE = (1.0, -0.125, 0.0026041646488010883, -2.1700563593185507e-05, 9.671927614363085e-08, -2.5440496931317114e-10)


def series(square, terms):
    total = terms[-1]
    for term in terms[-2::-1]:
        total = total * square + term
    return total


def cos_sin(angle):
    square = angle * angle
    sine = series(square, HALF_SINE) * angle
    twice = sine + sine
    return 1.0 - twice * sine, twice * series(square, HALF_COSINE)


def step_kernel(
    boxes,
    samps,
    partners,
    src_in,
    disp_in,
    octant_in,
    theta_index_in,
    theta_weight_in,
    phi_index_in,
    phi_weight_in,
    child,
    angle,
    table,
    field,
    wide,
    wide_out,
    grid_sum,
    theta_up,
    theta_down,
    src_rows,
    disp_rows,
    octant,
    theta_index_t,
    theta_weight_t,
    phi_index_t,
    phi_weight_t,
    *scratch,
):
    half = NT1 // 2
    width = 2 * NP1
    chunks = angle.shape[2] // LANES
    rows2 = angle.shape[1]
    sources = scratch[:chunks]
    operators = scratch[chunks : 2 * chunks]
    results = scratch[2 * chunks : 3 * chunks]
    outgoing = scratch[3 * chunks : 4 * chunks]
    incoming = scratch[4 * chunks : 5 * chunks]
    cosines = scratch[5 * chunks : 6 * chunks]
    sines = scratch[6 * chunks : 7 * chunks]
    (
        child_sem,
        angle_sem,
        load_sem,
        out_send,
        out_recv,
        box_send,
        box_recv,
        back_own,
        back_send,
        back_recv,
        small_sem,
    ) = scratch[7 * chunks :]
    per_device, parts = outgoing[0].shape[:2]
    kids = child.shape[0] // per_device
    per_row = width // LANES
    theta_rows = rows2 // samps
    edge = -(-(width // 2) // LANES) * LANES
    gap = edge - width // 2
    group = lax.axis_index("box")
    me = lax.axis_index("samp")
    bits = [1 << i for i in range(boxes.bit_length() - 1)][::-1]

    def mate(bit):
        return group + bit - 2 * bit * lax.rem(lax.div(group, bit), 2)

    def load(chunk):
        return pltpu.make_async_copy(
            table.at[:, :, :, pl.ds(chunk * LANES, LANES)], operators[chunk], load_sem.at[chunk]
        )

    def held_by(box, samp):
        return pl.ds((box * samps + samp) * per_device, per_device)

    last = chunks - 1
    middle = max(1, samps // 2)
    side = lax.div(me, middle)
    rim = max(1, samps // 4)

    def at_rim(peer):
        return jnp.logical_or(peer < rim, peer >= samps - rim)

    outer = at_rim(me)

    def apart(peer):
        return lax.rem(lax.div(peer, middle) + side, 2)

    def held_in(box, part):
        start = side if part == 0 else 1 - side
        return pl.ds((box * samps + start * middle) * per_device, middle * per_device)

    def keep(chunk):
        return pltpu.make_async_copy(
            outgoing[chunk].at[:, :, me], sources[chunk].at[held_by(group, me)], out_recv.at[chunk, 0]
        )

    def out_part(chunk, parent, peer):
        return pltpu.make_async_remote_copy(
            src_ref=outgoing[chunk].at[parent, :, peer],
            dst_ref=sources[chunk].at[(group * samps + me) * per_device + parent],
            send_sem=out_send.at[chunk],
            recv_sem=out_recv.at[chunk, apart(peer)],
            device_id=(group, peer),
            device_id_type=MESH,
        )

    def out_copy(chunk, peer):
        return pltpu.make_async_remote_copy(
            src_ref=outgoing[chunk].at[:, :, peer],
            dst_ref=sources[chunk].at[held_by(group, me)],
            send_sem=out_send.at[chunk],
            recv_sem=out_recv.at[chunk, apart(peer)],
            device_id=(group, peer),
            device_id_type=MESH,
        )

    def whole_back(chunk):
        return chunk == 0 and chunk < last

    def back_slot(chunk, slot):
        return 0 if whole_back(chunk) else chunk * per_device + slot

    def back_copy(chunk, peer):
        return pltpu.make_async_remote_copy(
            src_ref=results[chunk].at[peer],
            dst_ref=incoming[chunk].at[:, :, me],
            send_sem=back_send.at[chunk],
            recv_sem=back_recv.at[back_slot(chunk, 0)],
            device_id=(group, peer),
            device_id_type=MESH,
        )

    def back_part(chunk, slot, peer):
        return pltpu.make_async_remote_copy(
            src_ref=results[chunk].at[peer, slot],
            dst_ref=incoming[chunk].at[slot, :, me],
            send_sem=back_send.at[chunk],
            recv_sem=back_recv.at[back_slot(chunk, slot)],
            device_id=(group, peer),
            device_id_type=MESH,
        )

    def await_bytes(ref, sem):
        pltpu.make_async_copy(ref, ref, sem).wait()

    def back_keep(chunk):
        return pltpu.make_async_copy(
            results[chunk].at[me], incoming[chunk].at[:, :, me], back_own.at[chunk]
        )

    def box_plan():
        plan = []
        held = [0]
        for bit in bits:
            plan.append((bit, list(held)))
            held = held + [h + bit for h in held]
        return plan

    plan = box_plan()

    def owner_of(mask):
        spot = group
        for bit in bits:
            if mask & bit:
                spot = spot + bit - 2 * bit * lax.rem(lax.div(group, bit), 2)
        return spot

    def hop_slot(mask, part):
        return 0 if mask % 2 else mask - 1 + part

    def hop(chunk, bit, mask, part):
        spot = held_in(owner_of(mask), part)
        return pltpu.make_async_remote_copy(
            src_ref=sources[chunk].at[spot],
            dst_ref=sources[chunk].at[spot],
            send_sem=box_send.at[chunk],
            recv_sem=box_recv.at[chunk, hop_slot(mask + bit, part)],
            device_id=(mate(bit), me),
            device_id_type=MESH,
        )

    def load_angle(chunk):
        return pltpu.make_async_copy(
            angle.at[:, :, pl.ds(chunk * LANES, LANES)], cosines[chunk], angle_sem.at[chunk]
        )

    small = [
        pltpu.make_async_copy(source, place, small_sem.at[spot])
        for spot, (source, place) in enumerate(
            (
                (theta_index_in, theta_index_t),
                (theta_weight_in, theta_weight_t),
                (phi_index_in, phi_index_t),
                (phi_weight_in, phi_weight_t),
                (octant_in, octant),
                (src_in, src_rows),
                (disp_in, disp_rows),
            )
        )
    ]
    def load_child(parent):
        rows = pl.ds(parent * kids, kids)
        return pltpu.make_async_copy(child.at[rows], field.at[rows], child_sem.at[parent])

    def tile(parent, part, place):
        return (
            pl.ds(parent * kids, kids),
            pl.ds(place * parts + part, half, stride=per_row * parts),
            slice(None),
        )

    def build_theta():
        spot = iota((2 * half, rows2), 0)
        sample = jnp.where(spot < half, 2 * spot, 2 * (spot - half) + 1)
        narrow = stencil(sample, theta_index_t, theta_weight_t, 0)
        high, low = split(narrow.T)
        theta_up[:, : 2 * half] = high
        theta_up[:, 2 * half : 4 * half] = high
        theta_up[:, 4 * half :] = low
        high, low = split(narrow)
        theta_down[: 2 * half] = high
        theta_down[2 * half :] = low

    def turn(chunk):
        def one(spot, carry):
            cos_part, sin_part = cos_sin(cosines[chunk][spot])
            cosines[chunk][spot] = cos_part
            sines[chunk][spot] = sin_part
            return carry

        lax.fori_loop(0, cosines[chunk].shape[0], one, 0)

    def far(peer):
        return lax.div(peer, middle) != side

    def send_out(chunk, parent):
        spot = me - side * middle

        def near_one(step, carry):
            out_part(chunk, parent, side * middle + lax.rem(spot + step, middle)).start()
            return carry

        def far_one(step, carry):
            out_part(chunk, parent, (1 - side) * middle + lax.rem(spot + step, middle)).start()
            return carry

        lax.fori_loop(1, middle, near_one, 0)
        if chunk == 0:
            lax.fori_loop(0, middle, far_one, 0)

    def send_whole(chunk):
        def one(step, carry):
            out_copy(chunk, (1 - side) * middle + lax.rem(me - side * middle + 1 + step, middle)).start()
            return carry

        lax.fori_loop(0, middle, one, 0)

    def send_far(chunk):
        @pl.when(outer)
        def _():
            send_whole(chunk)

    def send_last(chunk):
        if chunk > 0:
            send_out(chunk, per_device - 1)

            @pl.when(jnp.logical_not(outer))
            def _():
                send_whole(chunk)

        keep(chunk).start()

    def aggregate(chunk, between):
        lanes = slice(chunk * LANES, (chunk + 1) * LANES)
        sample = iota((edge, LANES), 0)
        mats = []
        for shift in (0, gap):
            high, low = split(stencil(sample - shift, phi_index_t[:, lanes], phi_weight_t[:, lanes], 0))
            mats.append(jnp.concatenate([high, low], axis=1))

        def interpolate(parent):
            if chunk == 0:
                load_child(parent).wait()
            block = jnp.concatenate(
                [
                    jnp.concatenate(
                        [field[tile(parent, part, place)].reshape(kids * half, LANES) for place in range(per_row)],
                        axis=1,
                    )
                    for part in range(parts)
                ],
                axis=0,
            )
            pieces = []
            for mat, start in zip(mats, (0, width - edge)):
                high, low = split(block[:, start : start + edge])
                both = dot(high, mat)
                pieces.append(split(both[:, :LANES] + (both[:, LANES:] + dot(low, mat[:, :LANES]))))
            even, odd = pieces
            for slot, piece in enumerate((even[0], odd[0], even[1], odd[1], even[0], odd[0])):
                piece = piece.reshape(parts, kids, half, LANES)
                for part in range(parts):
                    wide[:, slot * half : (slot + 1) * half, part * LANES : (part + 1) * LANES] = piece[part]

        def first_half(turned, carry):
            part_of = lax.rem(turned + 1 - side, 2)
            rows = pl.ds(pl.multiple_of(part_of * (rows2 // 2), rows2 // 2), rows2 // 2)

            def one_octant(spot, inner):
                kid = 0
                for other in range(1, kids):
                    kid = jnp.where(octant[0, other] == spot, other, kid)
                fine = dot(theta_up[rows], wide[kid])
                real, imag = fine[:, :LANES], fine[:, LANES:]
                cos_part, sin_part = cos_sin(cosines[chunk][spot, rows])
                cosines[chunk][spot, rows] = cos_part
                sines[chunk][spot, rows] = sin_part
                grid_sum[0, rows] += real * cos_part - imag * sin_part
                grid_sum[1, rows] += real * sin_part + imag * cos_part
                return inner

            lax.fori_loop(0, kids, one_octant, 0, unroll=8)
            for owner in range(samps):

                @pl.when(part_of == owner // middle)
                def _():
                    for part in range(parts):
                        outgoing[chunk][0, part, owner] = grid_sum[
                            part, owner * theta_rows : (owner + 1) * theta_rows
                        ]

            @pl.when(turned == 0)
            def _():
                pl.semaphore_wait(barrier, samps - 1 + len(bits))

            def one(step, inner):
                peer = part_of * middle + step

                @pl.when(peer != me)
                def _():
                    out_part(chunk, 0, peer).start()

                return inner

            lax.fori_loop(0, middle, one, 0)
            return carry

        def one_parent(parent, carry):
            interpolate(parent)
            grid_sum[...] = jnp.zeros_like(grid_sum)

            if chunk > 0:

                @pl.when(parent > 0)
                def _():
                    send_out(chunk, parent - 1)

            if between:

                @pl.when(parent == per_device // 2)
                def _():
                    run(between)

            def one_child(kid, inner):
                spot = octant[parent, kid]
                fine = dot(theta_up[...], wide[kid])
                real, imag = fine[:, :LANES], fine[:, LANES:]
                cos_part = cosines[chunk][spot]
                sin_part = sines[chunk][spot]
                grid_sum[0] += real * cos_part - imag * sin_part
                grid_sum[1] += real * sin_part + imag * cos_part
                return inner

            lax.fori_loop(0, kids, one_child, 0, unroll=8)
            for part in range(parts):
                for owner in range(samps):
                    outgoing[chunk][parent, part, owner] = grid_sum[
                        part, owner * theta_rows : (owner + 1) * theta_rows
                    ]
            if chunk == 0:

                @pl.when(parent == per_device - 1)
                def _():
                    for later in range(chunks):
                        load(later).start()

                send_out(chunk, parent)
            return carry

        if chunk == 0:
            interpolate(0)
            grid_sum[...] = jnp.zeros_like(grid_sum)
            load_angle(chunk).wait()
            lax.fori_loop(0, 2, first_half, 0)
        lax.fori_loop(1 if chunk == 0 else 0, per_device, one_parent, 0)

    def disaggregate(chunk, first, between):
        rows = slice(chunk * LANES, (chunk + 1) * LANES)
        sample = iota((edge, LANES), 0)
        mats = []
        for shift in (0, gap):
            high, low = split(stencil(sample - shift, phi_index_t[:, rows], phi_weight_t[:, rows], 0).T)
            mats.append((jnp.concatenate([high, high], axis=0), low))

        def one_parent(parent, carry):
            returned_part(chunk, parent)
            for function in between:
                function(parent)
            for part in range(parts):
                for owner in range(samps):
                    grid_sum[part, owner * theta_rows : (owner + 1) * theta_rows] = incoming[chunk][
                        parent, part, owner
                    ]

            def one_child(kid, inner):
                spot = octant[parent, kid]
                real, imag = grid_sum[0], grid_sum[1]
                cos_part = cosines[chunk][spot]
                sin_part = sines[chunk][spot]
                turned = jnp.concatenate(
                    [real * cos_part + imag * sin_part, imag * cos_part - real * sin_part], axis=1
                )
                high, low = split(turned)
                both = dot(theta_down[...], high)
                narrow = both[: 2 * half] + (both[2 * half :] + dot(theta_down[: 2 * half], low))
                for place, piece in enumerate(split(narrow)):
                    for parity in range(2):
                        for part in range(parts):
                            wide_out[
                                parity, kid * parts + part, :, place * LANES : (place + 1) * LANES
                            ] = piece[parity * half : (parity + 1) * half, part * LANES : (part + 1) * LANES]
                return inner

            lax.fori_loop(0, kids, one_child, 0, unroll=8)
            ends = []
            for parity in range(2):
                flat = wide_out[parity].reshape(kids * parts * half, 2 * LANES)
                ends.append(dot(flat, mats[parity][0]) + dot(flat[:, :LANES], mats[parity][1]))
            left, right = ends
            shared = 2 * edge - width
            joined = jnp.concatenate(
                [left[:, : edge - shared], left[:, edge - shared :] + right[:, :shared], right[:, shared:]],
                axis=1,
            ).reshape(kids, parts, half, width)
            for part in range(parts):
                for place in range(per_row):
                    spot = tile(parent, part, place)
                    piece = joined[:, part, :, place * LANES : (place + 1) * LANES]
                    if first:
                        field[spot] = piece
                    else:
                        field[spot] = field[spot] + piece
            return carry

        lax.fori_loop(0, per_device, one_parent, 0)

    def share(chunk, part):
        await_bytes(sources[chunk].at[held_in(group, part)], out_recv.at[chunk, part])
        for bit, held in plan:
            hop(chunk, bit, 0, part).start()

    def pass_on(chunk, part):
        for position, (bit, held) in enumerate(plan):
            for mask in held:
                if mask == 0:
                    continue
                hop(chunk, bit, mask, part).start()
            if position + 1 < len(plan):
                for mask in [h + bit for h in held]:
                    await_bytes(sources[chunk].at[held_in(owner_of(mask), part)], box_recv.at[chunk, hop_slot(mask, part)])

    def back_far_part(chunk, slot, wanted=None):
        def one(step, carry):
            peer = (1 - side) * middle + step

            @pl.when(jnp.logical_or(wanted is None, at_rim(peer) == bool(wanted)))
            def _():
                back_part(chunk, slot, peer).start()

            return carry

        lax.fori_loop(0, middle, one, 0)

    def back_far(chunk):
        def one(slot, carry):
            back_far_part(chunk, slot)
            return carry

        def whole(step, carry):
            back_copy(chunk, (1 - side) * middle + lax.rem(me - side * middle + 1 + step, middle)).start()
            return carry

        @pl.when(outer)
        def _():
            if whole_back(chunk):
                lax.fori_loop(0, middle, whole, 0)
            else:
                lax.fori_loop(0, per_device, one, 0)

    def back_whole(chunk):
        def whole(step, carry):
            back_copy(chunk, (1 - side) * middle + lax.rem(me - side * middle + 1 + step, middle)).start()
            return carry

        @pl.when(jnp.logical_not(outer))
        def _():
            lax.fori_loop(0, middle, whole, 0)

    def back_last(parent):
        def late(slot):
            @pl.when(slot >= 0)
            def _():
                back_far_part(last, slot, False)

        @pl.when(outer)
        def _():
            for lead in range(OUTER_LAG):

                @pl.when(parent == 0)
                def _():
                    back_far_part(last, lead, True)

            @pl.when(parent + OUTER_LAG < per_device)
            def _():
                back_far_part(last, parent + OUTER_LAG, True)

            late(parent - OUTER_LAG)

            @pl.when(parent == per_device - 1)
            def _():
                for lag in range(OUTER_LAG):
                    late(per_device - OUTER_LAG + lag)

    def translate(chunk, between):
        await_bytes(sources[chunk].at[pl.ds(0, boxes // 2 * samps * per_device)], box_recv.at[chunk, 0])
        load(chunk).wait()

        def receivers(slot, carry):
            if between:

                @pl.when(slot == per_device // 2)
                def _():
                    run(between)

            def one(step, inner):
                peer = lax.rem(me + 1 + step, samps)
                row = (group * samps + peer) * per_device + slot
                real = jnp.zeros(results[chunk].shape[3:], jnp.float32)
                imag = jnp.zeros(results[chunk].shape[3:], jnp.float32)
                for q in range(partners):
                    source = src_rows[q, row]
                    which = disp_rows[q, row]
                    a = sources[chunk][source, 0]
                    b = sources[chunk][source, 1]
                    c = operators[chunk][which, 0]
                    d = operators[chunk][which, 1]
                    real = real + (c * a - d * b)
                    imag = imag + (c * b + d * a)
                results[chunk][peer, slot, 0] = real
                results[chunk][peer, slot, 1] = imag

                there = lax.rem(me + step, samps)

                distant = far(there)
                late = jnp.logical_and(distant, jnp.logical_not(at_rim(there))) if chunk == last else False

                @pl.when(jnp.logical_and(step > 0, jnp.logical_not(distant if whole_back(chunk) else jnp.logical_or(jnp.logical_and(outer, distant), late))))
                def _():
                    back_part(chunk, slot, there).start()

                if chunk == last:

                    @pl.when(jnp.logical_and(jnp.logical_and(late, slot >= INNER_LAG), jnp.logical_not(outer)))
                    def _():
                        back_part(chunk, slot - INNER_LAG, there).start()

                return inner

            lax.fori_loop(0, samps, one, 0)
            return carry

        lax.fori_loop(0, per_device, receivers, 0)
        if whole_back(chunk):
            back_whole(chunk)
        if chunk == last:

            @pl.when(jnp.logical_not(outer))
            def _():
                for slot in range(max(0, per_device - INNER_LAG), per_device):
                    back_far_part(chunk, slot, False)

    def returned_part(chunk, parent):
        if not whole_back(chunk):
            await_bytes(incoming[chunk].at[parent, :, pl.ds(0, samps - 1)], back_recv.at[back_slot(chunk, parent)])

    for copy in small[:5]:
        copy.start()
    load_child(0).start()
    load_angle(0).start()
    barrier = pltpu.get_barrier_semaphore()
    for step in range(1, samps):
        pl.semaphore_signal(barrier, inc=1, device_id=(group, lax.rem(me + step, samps)), device_id_type=MESH)
    for bit in bits:
        pl.semaphore_signal(barrier, inc=1, device_id=(mate(bit), me), device_id_type=MESH)
    for copy in small[5:]:
        copy.start()
    for copy in small[:5]:
        copy.wait()
    for parent in range(1, per_device):
        load_child(parent).start()
    for chunk in range(1, chunks):
        load_angle(chunk).start()
    build_theta()
    called = {(send_far, 0)}

    def fresh(*calls):
        left = [call for call in calls if 0 <= call[1] < chunks and call not in called]
        called.update(left)
        return left

    def run(calls):
        for function, *rest in calls:
            function(*rest)

    aggregate(0, [])
    for chunk in range(1, chunks):
        load_angle(chunk).wait()
        turn(chunk)
        send_last(chunk - 1)
        run(fresh((share, chunk - 2, 1)))
        if chunk > 1:
            run(fresh((send_far, chunk - 1)))
        aggregate(chunk, fresh((share, chunk - 1, 0), (pass_on, chunk - 2, 0)))
    send_last(last)
    for copy in small[5:]:
        copy.wait()
    for chunk in range(chunks):
        if chunk == last:
            run(fresh((send_far, last), (share, last, 0), (share, last, 1), (back_far, last - 2), (pass_on, last, 0)))
        run(fresh((share, chunk, 0), (pass_on, chunk, 0)))
        run(fresh((share, chunk, 1), (pass_on, chunk, 1)))
        if chunk:
            run(fresh((share, chunk + 1, 0)))
        if chunk:
            back_keep(chunk - 1).start()
        translate(chunk, fresh((share, chunk + 1, 1), (send_far, last)) if chunk + 1 < last else [])
    for chunk in range(last):
        run(fresh((back_far, chunk)))
        if chunk + 1 < last:
            run(fresh((back_far, chunk + 1)))
        back_keep(chunk).wait()
        if whole_back(chunk):
            await_bytes(incoming[chunk].at[:, :, pl.ds(0, samps - 1)], back_recv.at[back_slot(chunk, 0)])
        if chunk == 0:
            back_keep(last).start()
        disaggregate(chunk, chunk == 0, [back_last] if chunk + 1 == last else [])
    if last == 0:
        run(fresh((back_far, last)))
        back_keep(last).start()
    back_keep(last).wait()

    for chunk in range(chunks):
        await_bytes(outgoing[chunk].at[:, :, pl.ds(0, samps - 1)], out_send.at[chunk])
        await_bytes(sources[chunk].at[pl.ds(0, (boxes - 1) * samps * per_device)], box_send.at[chunk])
        if chunk < last:
            await_bytes(results[chunk].at[pl.ds(0, samps - 1)], back_send.at[chunk])
    disaggregate(last, last == 0, [])
    await_bytes(results[last].at[pl.ds(0, samps - 1)], back_send.at[last])


def local(
    boxes,
    samps,
    child_out,
    child_octant,
    theta_index,
    theta_weight,
    phi_index,
    phi_weight,
    shift_angle,
    partner_src,
    partner_disp,
    translation,
):
    child_count, parts, samples = child_out.shape
    parents, kids = child_octant.shape
    octant_count, rows2, cols2 = shift_angle.shape
    partners = partner_src.shape[1]
    theta_rows = rows2 // samps
    chunks = cols2 // LANES
    tiles = samples // LANES
    child = child_out.reshape(child_count, parts, tiles, LANES).transpose(0, 2, 1, 3)
    child = child.reshape(child_count, tiles * parts, LANES)
    block = (parents, parts, theta_rows, LANES)
    spread = (parents, parts, samps, theta_rows, LANES)
    turns = (octant_count, rows2, LANES)
    anywhere = pl.BlockSpec(memory_space=pl.ANY)
    vectors = pl.BlockSpec(memory_space=pltpu.VMEM)
    dma = pltpu.SemaphoreType.DMA

    def per_chunk(shape):
        return [pltpu.VMEM(shape, jnp.float32)] * chunks

    child_in = pl.pallas_call(
        functools.partial(step_kernel, boxes, samps, partners),
        out_shape=pltpu.VMEM(child.shape, jnp.float32),
        in_specs=[anywhere] * 10,
        out_specs=vectors,
        scratch_shapes=[
            pltpu.VMEM((kids, 3 * NT1, parts * LANES), jnp.bfloat16),
            pltpu.VMEM((2, kids * parts, NT1 // 2, 2 * LANES), jnp.bfloat16),
            pltpu.VMEM((parts, rows2, LANES), jnp.float32),
            pltpu.VMEM((rows2, 3 * NT1), jnp.bfloat16),
            pltpu.VMEM((2 * NT1, rows2), jnp.bfloat16),
            pltpu.SMEM(partner_src.shape[::-1], jnp.int32),
            pltpu.SMEM(partner_disp.shape[::-1], jnp.int32),
            pltpu.SMEM(child_octant.shape, jnp.int32),
            pltpu.VMEM(theta_index.shape[::-1], jnp.int32),
            pltpu.VMEM(theta_weight.shape[::-1], jnp.float32),
            pltpu.VMEM(phi_index.shape[::-1], jnp.int32),
            pltpu.VMEM(phi_weight.shape[::-1], jnp.float32),
        ]
        + per_chunk((boxes * samps * parents,) + block[1:])
        + per_chunk(translation.shape[:3] + (LANES,))
        + per_chunk((samps,) + block)
        + per_chunk(spread)
        + per_chunk(spread)
        + per_chunk(turns)
        + per_chunk(turns)
        + [
            dma((parents,)),
            dma((chunks,)),
            dma((chunks,)),
            dma((chunks,)),
            dma((chunks, 2)),
            dma((chunks,)),
            dma((chunks, boxes - 1)),
            dma((chunks,)),
            dma((chunks,)),
            dma((chunks * parents,)),
            dma((7,)),
        ],
        compiler_params=pltpu.CompilerParams(
            collective_id=0, has_side_effects=True, vmem_limit_bytes=VMEM_LIMIT
        ),
    )(
        partner_src.T,
        partner_disp.T,
        child_octant,
        theta_index.T,
        theta_weight.T,
        phi_index.T,
        phi_weight.T,
        child,
        shift_angle,
        translation,
    )
    child_in = child_in.reshape(child_count, tiles, parts, LANES).transpose(0, 2, 1, 3)
    return child_in.reshape(child_count, parts, samples)


def solution(mesh):
    in_specs = (
        P(("box", "samp"), None, None),
        P(("box", "samp"), None),
        P(),
        P(),
        P(),
        P(),
        P(),
        P(),
        P(),
        P(None, None, "samp", None),
    )
    out_specs = P(("box", "samp"), None, None)
    body = functools.partial(local, mesh.shape["box"], mesh.shape["samp"])
    return jax.shard_map(body, mesh=mesh, in_specs=in_specs, out_specs=out_specs, check_vma=False)
```

```python
import functools

import jax
import jax.numpy as jnp
from jax import lax
from jax.experimental import pallas as pl
from jax.experimental.pallas import tpu as pltpu
from jax.sharding import PartitionSpec as P

NT1 = 96
NP1 = 192
LANES = 128
MESH = pl.DeviceIdType.MESH
OUTER_LAG = 1
INNER_LAG = 1
VMEM_LIMIT = 56 * 1024 * 1024


def split(values):
    high = values.astype(jnp.bfloat16)
    low = (values - high.astype(jnp.float32)).astype(jnp.bfloat16)
    return high, low


def dot(left, right):
    return jnp.dot(left, right, preferred_element_type=jnp.float32)


def stencil(wanted, index, weight, axis):
    total = jnp.zeros(wanted.shape, jnp.float32)
    for j in range(index.shape[axis]):
        one = slice(j, j + 1)
        spot = (slice(None), one) if axis == 1 else (one, slice(None))
        total = total + jnp.where(wanted == index[spot], weight[spot], 0.0)
    return total


def iota(shape, axis):
    return lax.broadcasted_iota(jnp.int32, shape, axis)


HALF_SINE = (0.5, -0.02083333395421505, 0.00026041659293696284, -1.5500672816415317e-06, 5.376032508053186e-09, -1.1664790661169988e-11)
HALF_COSINE = (1.0, -0.125, 0.0026041646488010883, -2.1700563593185507e-05, 9.671927614363085e-08, -2.5440496931317114e-10)


def series(square, terms):
    total = terms[-1]
    for term in terms[-2::-1]:
        total = total * square + term
    return total


def cos_sin(angle):
    square = angle * angle
    sine = series(square, HALF_SINE) * angle
    twice = sine + sine
    return 1.0 - twice * sine, twice * series(square, HALF_COSINE)


def step_kernel(
    boxes,
    samps,
    partners,
    src_in,
    disp_in,
    octant_in,
    theta_index_in,
    theta_weight_in,
    phi_index_in,
    phi_weight_in,
    child,
    angle,
    table,
    field,
    wide,
    wide_out,
    grid_sum,
    theta_up,
    theta_down,
    src_rows,
    disp_rows,
    octant,
    theta_index_t,
    theta_weight_t,
    phi_index_t,
    phi_weight_t,
    *scratch,
):
    half = NT1 // 2
    width = 2 * NP1
    chunks = angle.shape[2] // LANES
    rows2 = angle.shape[1]
    sources = scratch[:chunks]
    operators = scratch[chunks : 2 * chunks]
    results = scratch[2 * chunks : 3 * chunks]
    outgoing = scratch[3 * chunks : 4 * chunks]
    incoming = scratch[4 * chunks : 5 * chunks]
    cosines = scratch[5 * chunks : 6 * chunks]
    sines = scratch[6 * chunks : 7 * chunks]
    (
        child_sem,
        angle_sem,
        load_sem,
        out_send,
        out_recv,
        box_send,
        box_recv,
        back_own,
        back_send,
        back_recv,
        small_sem,
    ) = scratch[7 * chunks :]
    per_device, parts = outgoing[0].shape[:2]
    kids = child.shape[0] // per_device
    per_row = width // LANES
    theta_rows = rows2 // samps
    edge = -(-(width // 2) // LANES) * LANES
    gap = edge - width // 2
    group = lax.axis_index("box")
    me = lax.axis_index("samp")
    bits = [1 << i for i in range(boxes.bit_length() - 1)][::-1]

    def mate(bit):
        return group + bit - 2 * bit * lax.rem(lax.div(group, bit), 2)

    def load(chunk):
        return pltpu.make_async_copy(
            table.at[:, :, :, pl.ds(chunk * LANES, LANES)], operators[chunk], load_sem.at[chunk]
        )

    def held_by(box, samp):
        return pl.ds((box * samps + samp) * per_device, per_device)

    last = chunks - 1
    middle = max(1, samps // 2)
    side = lax.div(me, middle)
    rim = max(1, samps // 4)

    def at_rim(peer):
        return jnp.logical_or(peer < rim, peer >= samps - rim)

    outer = at_rim(me)

    def apart(peer):
        return lax.rem(lax.div(peer, middle) + side, 2)

    def held_in(box, part):
        start = side if part == 0 else 1 - side
        return pl.ds((box * samps + start * middle) * per_device, middle * per_device)

    def keep(chunk):
        return pltpu.make_async_copy(
            outgoing[chunk].at[:, :, me], sources[chunk].at[held_by(group, me)], out_recv.at[chunk, 0]
        )

    def out_part(chunk, parent, peer):
        return pltpu.make_async_remote_copy(
            src_ref=outgoing[chunk].at[parent, :, peer],
            dst_ref=sources[chunk].at[(group * samps + me) * per_device + parent],
            send_sem=out_send.at[chunk],
            recv_sem=out_recv.at[chunk, apart(peer)],
            device_id=(group, peer),
            device_id_type=MESH,
        )

    def out_copy(chunk, peer):
        return pltpu.make_async_remote_copy(
            src_ref=outgoing[chunk].at[:, :, peer],
            dst_ref=sources[chunk].at[held_by(group, me)],
            send_sem=out_send.at[chunk],
            recv_sem=out_recv.at[chunk, apart(peer)],
            device_id=(group, peer),
            device_id_type=MESH,
        )

    def whole_back(chunk):
        return chunk < last

    def back_slot(chunk, slot):
        return chunk if whole_back(chunk) else last + slot

    def back_copy(chunk, peer):
        return pltpu.make_async_remote_copy(
            src_ref=results[chunk].at[peer],
            dst_ref=incoming[chunk].at[:, :, me],
            send_sem=back_send.at[chunk],
            recv_sem=back_recv.at[back_slot(chunk, 0)],
            device_id=(group, peer),
            device_id_type=MESH,
        )

    def back_part(chunk, slot, peer):
        return pltpu.make_async_remote_copy(
            src_ref=results[chunk].at[peer, slot],
            dst_ref=incoming[chunk].at[slot, :, me],
            send_sem=back_send.at[chunk],
            recv_sem=back_recv.at[back_slot(chunk, slot)],
            device_id=(group, peer),
            device_id_type=MESH,
        )

    def await_bytes(ref, sem):
        pltpu.make_async_copy(ref, ref, sem).wait()

    def back_keep(chunk):
        return pltpu.make_async_copy(
            results[chunk].at[me], incoming[chunk].at[:, :, me], back_own.at[chunk]
        )

    def box_plan():
        plan = []
        held = [0]
        for bit in bits:
            plan.append((bit, list(held)))
            held = held + [h + bit for h in held]
        return plan

    plan = box_plan()

    def owner_of(mask):
        spot = group
        for bit in bits:
            if mask & bit:
                spot = spot + bit - 2 * bit * lax.rem(lax.div(group, bit), 2)
        return spot

    def hop_slot(mask, part):
        return 0 if mask % 2 else mask - 1 + part

    def hop(chunk, bit, mask, part):
        spot = held_in(owner_of(mask), part)
        return pltpu.make_async_remote_copy(
            src_ref=sources[chunk].at[spot],
            dst_ref=sources[chunk].at[spot],
            send_sem=box_send.at[chunk],
            recv_sem=box_recv.at[chunk, hop_slot(mask + bit, part)],
            device_id=(mate(bit), me),
            device_id_type=MESH,
        )

    def load_angle(chunk):
        return pltpu.make_async_copy(
            angle.at[:, :, pl.ds(chunk * LANES, LANES)], cosines[chunk], angle_sem.at[chunk]
        )

    small = [
        pltpu.make_async_copy(source, place, small_sem.at[spot])
        for spot, (source, place) in enumerate(
            (
                (theta_index_in, theta_index_t),
                (theta_weight_in, theta_weight_t),
                (phi_index_in, phi_index_t),
                (phi_weight_in, phi_weight_t),
                (octant_in, octant),
                (src_in, src_rows),
                (disp_in, disp_rows),
            )
        )
    ]
    def load_child(parent):
        rows = pl.ds(parent * kids, kids)
        return pltpu.make_async_copy(child.at[rows], field.at[rows], child_sem.at[parent])

    def tile(parent, part, place):
        return (
            pl.ds(parent * kids, kids),
            pl.ds(place * parts + part, half, stride=per_row * parts),
            slice(None),
        )

    def build_theta():
        spot = iota((2 * half, rows2), 0)
        sample = jnp.where(spot < half, 2 * spot, 2 * (spot - half) + 1)
        narrow = stencil(sample, theta_index_t, theta_weight_t, 0)
        high, low = split(narrow.T)
        theta_up[:, : 2 * half] = high
        theta_up[:, 2 * half : 4 * half] = high
        theta_up[:, 4 * half :] = low
        high, low = split(narrow)
        theta_down[: 2 * half] = high
        theta_down[2 * half :] = low

    def turn(chunk):
        def one(spot, carry):
            cos_part, sin_part = cos_sin(cosines[chunk][spot])
            cosines[chunk][spot] = cos_part
            sines[chunk][spot] = sin_part
            return carry

        lax.fori_loop(0, cosines[chunk].shape[0], one, 0)

    def far(peer):
        return lax.div(peer, middle) != side

    def send_out(chunk, parent):
        spot = me - side * middle

        def near_one(step, carry):
            out_part(chunk, parent, side * middle + lax.rem(spot + step, middle)).start()
            return carry

        def far_one(step, carry):
            out_part(chunk, parent, (1 - side) * middle + lax.rem(spot + step, middle)).start()
            return carry

        lax.fori_loop(1, middle, near_one, 0)
        if chunk == 0:
            lax.fori_loop(0, middle, far_one, 0)

    def send_whole(chunk):
        def one(step, carry):
            out_copy(chunk, (1 - side) * middle + lax.rem(me - side * middle + 1 + step, middle)).start()
            return carry

        lax.fori_loop(0, middle, one, 0)

    def send_far(chunk):
        @pl.when(outer)
        def _():
            send_whole(chunk)

    def send_last(chunk):
        if chunk > 0:
            send_out(chunk, per_device - 1)

            @pl.when(jnp.logical_not(outer))
            def _():
                send_whole(chunk)

        keep(chunk).start()

    def aggregate(chunk, between):
        lanes = slice(chunk * LANES, (chunk + 1) * LANES)
        sample = iota((edge, LANES), 0)
        mats = []
        for shift in (0, gap):
            high, low = split(stencil(sample - shift, phi_index_t[:, lanes], phi_weight_t[:, lanes], 0))
            mats.append(jnp.concatenate([high, low], axis=1))

        def interpolate(parent):
            if chunk == 0:
                load_child(parent).wait()
            block = jnp.concatenate(
                [
                    jnp.concatenate(
                        [field[tile(parent, part, place)].reshape(kids * half, LANES) for place in range(per_row)],
                        axis=1,
                    )
                    for part in range(parts)
                ],
                axis=0,
            )
            pieces = []
            for mat, start in zip(mats, (0, width - edge)):
                high, low = split(block[:, start : start + edge])
                both = dot(high, mat)
                pieces.append(split(both[:, :LANES] + (both[:, LANES:] + dot(low, mat[:, :LANES]))))
            even, odd = pieces
            for slot, piece in enumerate((even[0], odd[0], even[1], odd[1], even[0], odd[0])):
                piece = piece.reshape(parts, kids, half, LANES)
                for part in range(parts):
                    wide[:, slot * half : (slot + 1) * half, part * LANES : (part + 1) * LANES] = piece[part]

        def first_half(turned, carry):
            part_of = lax.rem(turned + 1 - side, 2)
            rows = pl.ds(pl.multiple_of(part_of * (rows2 // 2), rows2 // 2), rows2 // 2)

            def one_octant(spot, inner):
                kid = 0
                for other in range(1, kids):
                    kid = jnp.where(octant[0, other] == spot, other, kid)
                fine = dot(theta_up[rows], wide[kid])
                real, imag = fine[:, :LANES], fine[:, LANES:]
                cos_part, sin_part = cos_sin(cosines[chunk][spot, rows])
                cosines[chunk][spot, rows] = cos_part
                sines[chunk][spot, rows] = sin_part
                grid_sum[0, rows] += real * cos_part - imag * sin_part
                grid_sum[1, rows] += real * sin_part + imag * cos_part
                return inner

            lax.fori_loop(0, kids, one_octant, 0, unroll=8)
            for owner in range(samps):

                @pl.when(part_of == owner // middle)
                def _():
                    for part in range(parts):
                        outgoing[chunk][0, part, owner] = grid_sum[
                            part, owner * theta_rows : (owner + 1) * theta_rows
                        ]

            @pl.when(turned == 0)
            def _():
                pl.semaphore_wait(barrier, samps - 1 + len(bits))

            def one(step, inner):
                peer = part_of * middle + step

                @pl.when(peer != me)
                def _():
                    out_part(chunk, 0, peer).start()

                return inner

            lax.fori_loop(0, middle, one, 0)
            return carry

        def one_parent(parent, carry):
            interpolate(parent)
            grid_sum[...] = jnp.zeros_like(grid_sum)

            if chunk > 0:

                @pl.when(parent > 0)
                def _():
                    send_out(chunk, parent - 1)

            if between:

                @pl.when(parent == per_device // 2)
                def _():
                    run(between)

            def one_child(kid, inner):
                spot = octant[parent, kid]
                fine = dot(theta_up[...], wide[kid])
                real, imag = fine[:, :LANES], fine[:, LANES:]
                cos_part = cosines[chunk][spot]
                sin_part = sines[chunk][spot]
                grid_sum[0] += real * cos_part - imag * sin_part
                grid_sum[1] += real * sin_part + imag * cos_part
                return inner

            lax.fori_loop(0, kids, one_child, 0, unroll=8)
            for part in range(parts):
                for owner in range(samps):
                    outgoing[chunk][parent, part, owner] = grid_sum[
                        part, owner * theta_rows : (owner + 1) * theta_rows
                    ]
            if chunk == 0:

                @pl.when(parent == per_device - 1)
                def _():
                    for later in range(chunks):
                        load(later).start()

                send_out(chunk, parent)
            return carry

        if chunk == 0:
            interpolate(0)
            grid_sum[...] = jnp.zeros_like(grid_sum)
            load_angle(chunk).wait()
            lax.fori_loop(0, 2, first_half, 0)
        lax.fori_loop(1 if chunk == 0 else 0, per_device, one_parent, 0)

    def disaggregate(chunk, first, between):
        rows = slice(chunk * LANES, (chunk + 1) * LANES)
        sample = iota((edge, LANES), 0)
        mats = []
        for shift in (0, gap):
            high, low = split(stencil(sample - shift, phi_index_t[:, rows], phi_weight_t[:, rows], 0).T)
            mats.append((jnp.concatenate([high, high], axis=0), low))

        def one_parent(parent, carry):
            returned_part(chunk, parent)
            for function in between:
                function(parent)
            for part in range(parts):
                for owner in range(samps):
                    grid_sum[part, owner * theta_rows : (owner + 1) * theta_rows] = incoming[chunk][
                        parent, part, owner
                    ]

            def one_child(kid, inner):
                spot = octant[parent, kid]
                real, imag = grid_sum[0], grid_sum[1]
                cos_part = cosines[chunk][spot]
                sin_part = sines[chunk][spot]
                turned = jnp.concatenate(
                    [real * cos_part + imag * sin_part, imag * cos_part - real * sin_part], axis=1
                )
                high, low = split(turned)
                both = dot(theta_down[...], high)
                narrow = both[: 2 * half] + (both[2 * half :] + dot(theta_down[: 2 * half], low))
                for place, piece in enumerate(split(narrow)):
                    for parity in range(2):
                        for part in range(parts):
                            wide_out[
                                parity, kid * parts + part, :, place * LANES : (place + 1) * LANES
                            ] = piece[parity * half : (parity + 1) * half, part * LANES : (part + 1) * LANES]
                return inner

            lax.fori_loop(0, kids, one_child, 0, unroll=8)
            ends = []
            for parity in range(2):
                flat = wide_out[parity].reshape(kids * parts * half, 2 * LANES)
                ends.append(dot(flat, mats[parity][0]) + dot(flat[:, :LANES], mats[parity][1]))
            left, right = ends
            shared = 2 * edge - width
            joined = jnp.concatenate(
                [left[:, : edge - shared], left[:, edge - shared :] + right[:, :shared], right[:, shared:]],
                axis=1,
            ).reshape(kids, parts, half, width)
            for part in range(parts):
                for place in range(per_row):
                    spot = tile(parent, part, place)
                    piece = joined[:, part, :, place * LANES : (place + 1) * LANES]
                    if first:
                        field[spot] = piece
                    else:
                        field[spot] = field[spot] + piece
            return carry

        lax.fori_loop(0, per_device, one_parent, 0)

    def share(chunk, part):
        await_bytes(sources[chunk].at[held_in(group, part)], out_recv.at[chunk, part])
        for bit, held in plan:
            hop(chunk, bit, 0, part).start()

    def pass_on(chunk, part):
        for position, (bit, held) in enumerate(plan):
            for mask in held:
                if mask == 0:
                    continue
                hop(chunk, bit, mask, part).start()
            if position + 1 < len(plan):
                for mask in [h + bit for h in held]:
                    await_bytes(sources[chunk].at[held_in(owner_of(mask), part)], box_recv.at[chunk, hop_slot(mask, part)])

    def back_far_part(chunk, slot, wanted=None):
        def one(step, carry):
            peer = (1 - side) * middle + step

            @pl.when(jnp.logical_or(wanted is None, at_rim(peer) == bool(wanted)))
            def _():
                back_part(chunk, slot, peer).start()

            return carry

        lax.fori_loop(0, middle, one, 0)

    def back_far(chunk):
        def one(slot, carry):
            back_far_part(chunk, slot)
            return carry

        def whole(step, carry):
            back_copy(chunk, (1 - side) * middle + lax.rem(me - side * middle + 1 + step, middle)).start()
            return carry

        @pl.when(outer)
        def _():
            if whole_back(chunk):
                lax.fori_loop(0, middle, whole, 0)
            else:
                lax.fori_loop(0, per_device, one, 0)

    def back_whole(chunk):
        def whole(step, carry):
            back_copy(chunk, (1 - side) * middle + lax.rem(me - side * middle + 1 + step, middle)).start()
            return carry

        @pl.when(jnp.logical_not(outer))
        def _():
            lax.fori_loop(0, middle, whole, 0)

    def back_last(parent):
        def late(slot):
            @pl.when(slot >= 0)
            def _():
                back_far_part(last, slot, False)

        @pl.when(outer)
        def _():
            for lead in range(OUTER_LAG):

                @pl.when(parent == 0)
                def _():
                    back_far_part(last, lead, True)

            @pl.when(parent + OUTER_LAG < per_device)
            def _():
                back_far_part(last, parent + OUTER_LAG, True)

            late(parent - OUTER_LAG)

            @pl.when(parent == per_device - 1)
            def _():
                for lag in range(OUTER_LAG):
                    late(per_device - OUTER_LAG + lag)

    def translate(chunk, between):
        await_bytes(sources[chunk].at[pl.ds(0, boxes // 2 * samps * per_device)], box_recv.at[chunk, 0])
        load(chunk).wait()

        def receivers(slot, carry):
            if between:

                @pl.when(slot == per_device // 2)
                def _():
                    run(between)

            def one(step, inner):
                peer = lax.rem(me + 1 + step, samps)
                row = (group * samps + peer) * per_device + slot
                real = jnp.zeros(results[chunk].shape[3:], jnp.float32)
                imag = jnp.zeros(results[chunk].shape[3:], jnp.float32)
                for q in range(partners):
                    source = src_rows[q, row]
                    which = disp_rows[q, row]
                    a = sources[chunk][source, 0]
                    b = sources[chunk][source, 1]
                    c = operators[chunk][which, 0]
                    d = operators[chunk][which, 1]
                    real = real + (c * a - d * b)
                    imag = imag + (c * b + d * a)
                results[chunk][peer, slot, 0] = real
                results[chunk][peer, slot, 1] = imag

                there = lax.rem(me + step, samps)

                distant = far(there)
                late = jnp.logical_and(distant, jnp.logical_not(at_rim(there))) if chunk == last else False

                @pl.when(jnp.logical_and(step > 0, jnp.logical_not(distant if whole_back(chunk) else jnp.logical_or(jnp.logical_and(outer, distant), late))))
                def _():
                    back_part(chunk, slot, there).start()

                if chunk == last:

                    @pl.when(jnp.logical_and(jnp.logical_and(late, slot >= INNER_LAG), jnp.logical_not(outer)))
                    def _():
                        back_part(chunk, slot - INNER_LAG, there).start()

                return inner

            lax.fori_loop(0, samps, one, 0)
            return carry

        lax.fori_loop(0, per_device, receivers, 0)
        if whole_back(chunk):
            back_whole(chunk)
        if chunk == last:

            @pl.when(jnp.logical_not(outer))
            def _():
                for slot in range(max(0, per_device - INNER_LAG), per_device):
                    back_far_part(chunk, slot, False)

    def returned_part(chunk, parent):
        if not whole_back(chunk):
            await_bytes(incoming[chunk].at[parent, :, pl.ds(0, samps - 1)], back_recv.at[back_slot(chunk, parent)])

    for copy in small[:5]:
        copy.start()
    load_child(0).start()
    load_angle(0).start()
    barrier = pltpu.get_barrier_semaphore()
    for step in range(1, samps):
        pl.semaphore_signal(barrier, inc=1, device_id=(group, lax.rem(me + step, samps)), device_id_type=MESH)
    for bit in bits:
        pl.semaphore_signal(barrier, inc=1, device_id=(mate(bit), me), device_id_type=MESH)
    for copy in small[5:]:
        copy.start()
    for copy in small[:5]:
        copy.wait()
    for parent in range(1, per_device):
        load_child(parent).start()
    for chunk in range(1, chunks):
        load_angle(chunk).start()
    build_theta()
    called = {(send_far, 0)}

    def fresh(*calls):
        left = [call for call in calls if 0 <= call[1] < chunks and call not in called]
        called.update(left)
        return left

    def run(calls):
        for function, *rest in calls:
            function(*rest)

    aggregate(0, [])
    for chunk in range(1, chunks):
        load_angle(chunk).wait()
        turn(chunk)
        send_last(chunk - 1)
        run(fresh((share, chunk - 2, 1)))
        if chunk > 1:
            run(fresh((send_far, chunk - 1)))
        aggregate(chunk, fresh((share, chunk - 1, 0), (pass_on, chunk - 2, 0)))
    send_last(last)
    for copy in small[5:]:
        copy.wait()
    for chunk in range(chunks):
        if chunk == last:
            run(fresh((send_far, last), (share, last, 0), (share, last, 1), (back_far, last - 2), (pass_on, last, 0)))
        run(fresh((share, chunk, 0), (pass_on, chunk, 0)))
        run(fresh((share, chunk, 1), (pass_on, chunk, 1)))
        if chunk:
            run(fresh((share, chunk + 1, 0)))
        if chunk:
            back_keep(chunk - 1).start()
        translate(chunk, fresh((share, chunk + 1, 1), (send_far, last)) if chunk + 1 < last else [])
    for chunk in range(last):
        run(fresh((back_far, chunk)))
        if chunk + 1 < last:
            run(fresh((back_far, chunk + 1)))
        back_keep(chunk).wait()
        if whole_back(chunk):
            await_bytes(incoming[chunk].at[:, :, pl.ds(0, samps - 1)], back_recv.at[back_slot(chunk, 0)])
        if chunk == 0:
            back_keep(last).start()
        disaggregate(chunk, chunk == 0, [back_last] if chunk + 1 == last else [])
    if last == 0:
        run(fresh((back_far, last)))
        back_keep(last).start()
    back_keep(last).wait()

    for chunk in range(chunks):
        await_bytes(outgoing[chunk].at[:, :, pl.ds(0, samps - 1)], out_send.at[chunk])
        await_bytes(sources[chunk].at[pl.ds(0, (boxes - 1) * samps * per_device)], box_send.at[chunk])
        if chunk < last:
            await_bytes(results[chunk].at[pl.ds(0, samps - 1)], back_send.at[chunk])
    disaggregate(last, last == 0, [])
    await_bytes(results[last].at[pl.ds(0, samps - 1)], back_send.at[last])


def local(
    boxes,
    samps,
    child_out,
    child_octant,
    theta_index,
    theta_weight,
    phi_index,
    phi_weight,
    shift_angle,
    partner_src,
    partner_disp,
    translation,
):
    child_count, parts, samples = child_out.shape
    parents, kids = child_octant.shape
    octant_count, rows2, cols2 = shift_angle.shape
    partners = partner_src.shape[1]
    theta_rows = rows2 // samps
    chunks = cols2 // LANES
    tiles = samples // LANES
    child = child_out.reshape(child_count, parts, tiles, LANES).transpose(0, 2, 1, 3)
    child = child.reshape(child_count, tiles * parts, LANES)
    block = (parents, parts, theta_rows, LANES)
    spread = (parents, parts, samps, theta_rows, LANES)
    turns = (octant_count, rows2, LANES)
    anywhere = pl.BlockSpec(memory_space=pl.ANY)
    vectors = pl.BlockSpec(memory_space=pltpu.VMEM)
    dma = pltpu.SemaphoreType.DMA

    def per_chunk(shape):
        return [pltpu.VMEM(shape, jnp.float32)] * chunks

    child_in = pl.pallas_call(
        functools.partial(step_kernel, boxes, samps, partners),
        out_shape=pltpu.VMEM(child.shape, jnp.float32),
        in_specs=[anywhere] * 10,
        out_specs=vectors,
        scratch_shapes=[
            pltpu.VMEM((kids, 3 * NT1, parts * LANES), jnp.bfloat16),
            pltpu.VMEM((2, kids * parts, NT1 // 2, 2 * LANES), jnp.bfloat16),
            pltpu.VMEM((parts, rows2, LANES), jnp.float32),
            pltpu.VMEM((rows2, 3 * NT1), jnp.bfloat16),
            pltpu.VMEM((2 * NT1, rows2), jnp.bfloat16),
            pltpu.SMEM(partner_src.shape[::-1], jnp.int32),
            pltpu.SMEM(partner_disp.shape[::-1], jnp.int32),
            pltpu.SMEM(child_octant.shape, jnp.int32),
            pltpu.VMEM(theta_index.shape[::-1], jnp.int32),
            pltpu.VMEM(theta_weight.shape[::-1], jnp.float32),
            pltpu.VMEM(phi_index.shape[::-1], jnp.int32),
            pltpu.VMEM(phi_weight.shape[::-1], jnp.float32),
        ]
        + per_chunk((boxes * samps * parents,) + block[1:])
        + per_chunk(translation.shape[:3] + (LANES,))
        + per_chunk((samps,) + block)
        + per_chunk(spread)
        + per_chunk(spread)
        + per_chunk(turns)
        + per_chunk(turns)
        + [
            dma((parents,)),
            dma((chunks,)),
            dma((chunks,)),
            dma((chunks,)),
            dma((chunks, 2)),
            dma((chunks,)),
            dma((chunks, boxes - 1)),
            dma((chunks,)),
            dma((chunks,)),
            dma((chunks - 1 + parents,)),
            dma((7,)),
        ],
        compiler_params=pltpu.CompilerParams(
            collective_id=0, has_side_effects=True, vmem_limit_bytes=VMEM_LIMIT
        ),
    )(
        partner_src.T,
        partner_disp.T,
        child_octant,
        theta_index.T,
        theta_weight.T,
        phi_index.T,
        phi_weight.T,
        child,
        shift_angle,
        translation,
    )
    child_in = child_in.reshape(child_count, tiles, parts, LANES).transpose(0, 2, 1, 3)
    return child_in.reshape(child_count, parts, samples)


def solution(mesh):
    in_specs = (
        P(("box", "samp"), None, None),
        P(("box", "samp"), None),
        P(),
        P(),
        P(),
        P(),
        P(),
        P(),
        P(),
        P(None, None, "samp", None),
    )
    out_specs = P(("box", "samp"), None, None)
    body = functools.partial(local, mesh.shape["box"], mesh.shape["samp"])
    return jax.shard_map(body, mesh=mesh, in_specs=in_specs, out_specs=out_specs, check_vma=False)
```
